128 devices in a mesh: frame: 16 (over y, x), tensor: 8 (over z, core).
Axes of the slice: x: 4, y: 4, z: 4, core: 2. Of those that a mesh axis runs over, the one named last changes fastest.
Arguments:
- latents: bfloat16 [8192, 5120], P('frame', 'tensor'), may hold values from -6 to 6
- w_query: bfloat16 [5120, 3072], P(None, 'tensor'), may hold values from -0.078125 to 0.078125
- w_key: bfloat16 [5120, 3072], P(None, 'tensor'), may hold values from -0.078125 to 0.078125
- w_value: bfloat16 [5120, 3072], P(None, 'tensor'), may hold values from -0.078125 to 0.078125
- w_out: bfloat16 [3072, 5120], P('tensor'), may hold values from -0.109375 to 0.109375
- query_gain: float32 [24, 128], P('tensor'), may hold values from 0.5 to 14, as said below
- key_gain: float32 [24, 128], P('tensor'), may hold values from 0.5 to 14, as said below
- mod_table: float32 [16, 3, 5120], replicated, may hold values from -3 to 3
- levels: int32 [16], P('frame'), may hold values from 0 to 15
- span_counts: int32 [16], replicated, may hold values from 1 to 512, 6144 in all
- block_mask: int32 [16, 16], P('frame'), may hold values 0 or 1
- span_order: int32 [16], replicated, may hold values from 0 to 15, each once
Outputs:
- updated: bfloat16 [8192, 5120], P('frame', 'tensor')
The draws below stay inside these ranges and needn't reach their ends.
Inputs may be any that keep to these rules, and one draw needn't show every extreme that they name: `query_gain`: gains are positive. `key_gain`: gains are positive. `span_order`: each rank appears once.
All inputs are finite; a program needn't handle non-finite values. No bound on the sum of `block_mask` on one device may be relied on, other than what follows from the above.
Results may differ from the reference program's by a relative error of at most 0.012.
The reference program's roundings to bfloat16 on the way count: a program that leaves them out, or rounds other values in their place, can miss the bound.
Values may be sent and summed in bfloat16 or wider, within the bound.
No kernel may reach another device: no remote copies, remote signals or barrier semaphores. Data moves between devices by JAX's collectives and lax.ppermute only.
A program may use at most 128 MiB of HBM per device.

```python
import math
import jax
import jax.numpy as jnp
import numpy as np
from jax import lax

D = 5120
HEADS = 24
HEAD_DIM = 128
LEVELS = 16
ROWS = 512
SPANS = 16
TOKENS = 8192
N_TENSOR = 8


def gain_values(key, salt):
    own_key = jax.random.fold_in(key, salt)
    gain_table = jnp.exp(jax.random.uniform(own_key, (HEADS, HEAD_DIM), jnp.float32, math.log(0.5), math.log(2.0)))
    return gain_table


def draw_query_gain(key, part):
    return gain_values(key, 11)


def draw_key_gain(key, part):
    return gain_values(key, 23)


def place_ends(values, stream_key, least, largest):
    index_at = [jax.random.randint(jax.random.fold_in(stream_key, axis), (), 0, length) for axis, length in enumerate(values.shape)]
    main_axis = values.shape.index(max(values.shape))
    beside = index_at[:main_axis] + [(index_at[main_axis] + 1) % values.shape[main_axis]] + index_at[main_axis + 1:]
    return values.at[tuple(index_at)].set(least).at[tuple(beside)].set(largest)


def shard_levels(rng, extent, split, smallest, top_value):
    level, own = 1.0, jax.random.fold_in(rng, 6)
    for dim, parts in split:
        steps = jnp.exp(jax.random.uniform(jax.random.fold_in(own, dim), (parts,), jnp.float32, smallest / len(split), top_value / len(split)))
        level = level * jnp.repeat(steps, extent[dim] // parts).reshape([-1 if axis == dim else 1 for axis in range(len(extent))])
    return level


def profile(amount, total, reach, slope):
    portions = [(1 << 20) // math.isqrt(standing ** slope) + 1 for standing in range(2, amount + 1)]
    spare, holding = total - reach - (amount - 1), [1] * (amount - 1)
    while spare > 0:
        movable = [i for i in range(amount - 1) if holding[i] < reach]
        mass, remaining = sum([portions[i] for i in movable]), spare
        for i in movable:
            addition = min(reach - holding[i], max(1, remaining * portions[i] // mass), spare)
            holding[i] = holding[i] + addition
            spare = spare - addition
    return np.array([reach] + holding)


def uneven_parts(rng, number_of, total, reach, skew):
    if number_of == 2:
        one = jax.random.randint(rng, (), max(1, total - reach), min(reach, total - 1) + 1)
        return jnp.stack([one, total - one])
    sizes = jnp.asarray(profile(number_of, total, reach, skew), jnp.int32)
    twos = (number_of - 1) // 2
    giver, taker = sizes[1:1 + 2 * twos:2], sizes[2:2 + 2 * twos:2]
    slack = jnp.minimum(giver - 1, reach - taker)
    moved = jax.random.randint(jax.random.fold_in(rng, 1), (twos,), 0, 1 << 20) % (slack + 1)
    sizes = sizes.at[1:1 + 2 * twos:2].set(giver - moved).at[2:2 + 2 * twos:2].set(taker + moved)
    return sizes[jax.random.permutation(jax.random.fold_in(rng, 2), number_of)]


def noise(key, extent, deviation, most, split=(), kind=jnp.bfloat16):
    entries = jax.random.normal(key, extent, jnp.float32) * deviation
    if len(split) > 0:
        entries = shard_levels(key, extent, split, -0.22, 0.18) * entries
    return jnp.clip(entries, min=-most, max=most).astype(kind)


def setup_inputs(seed: int = 0) -> dict:
    seeds = jax.random.split(jax.random.key(seed), 13)
    latents = noise(seeds[0], (TOKENS, D), 1.0, 6.0, ((0, 16), (1, 8)))
    w_query = noise(seeds[1], (D, HEADS * HEAD_DIM), D ** -0.5, 0.078125, ((1, 8),))
    w_key = noise(seeds[2], (D, HEADS * HEAD_DIM), D ** -0.5, 0.078125, ((1, 8),))
    w_value = noise(seeds[3], (D, HEADS * HEAD_DIM), D ** -0.5, 0.078125, ((1, 8),))
    w_out = noise(seeds[4], (HEADS * HEAD_DIM, D), (HEADS * HEAD_DIM) ** -0.5, 0.109375, ((0, 8),))
    query_gain = draw_query_gain(jax.random.fold_in(seeds[12], 71), 0)
    key_gain = draw_key_gain(jax.random.fold_in(seeds[12], 71), 0)
    mod_table = noise(seeds[7], (LEVELS, 3, D), 0.5, 3.0, (), jnp.float32)
    levels = place_ends(jax.random.randint(seeds[8], (SPANS,), 0, LEVELS), jax.random.fold_in(seeds[8], 1), 0, LEVELS - 1).astype(jnp.int32)
    span_counts = uneven_parts(seeds[9], SPANS, 3 * ROWS * SPANS // 4, ROWS, 1).astype(jnp.int32)
    block_mask = place_ends((jax.random.randint(seeds[10], (SPANS, SPANS), 0, 4) < 3).astype(jnp.int32), jax.random.fold_in(seeds[10], 1), 0, 1)
    span_order = jax.random.permutation(seeds[11], SPANS).astype(jnp.int32)
    return dict(latents=latents, w_query=w_query, w_key=w_key, w_value=w_value, w_out=w_out, query_gain=query_gain, key_gain=key_gain, mod_table=mod_table, levels=levels, span_counts=span_counts, block_mask=block_mask, span_order=span_order)


EPSILON = 1e-06
NEG_FILL = -1e+30

def head_norm(projection, gain_table):
    shaped = projection.reshape(TOKENS, HEADS, HEAD_DIM)
    scaled = shaped * lax.rsqrt(lax.optimization_barrier(jnp.mean(shaped * shaped, axis=-1, keepdims=True)) + EPSILON) * gain_table
    return scaled.astype(jnp.bfloat16)

def reference(latents, w_query, w_key, w_value, w_out, query_gain, key_gain, mod_table, levels, span_counts, block_mask, span_order):
    modulation = mod_table[levels]
    shift = jnp.repeat(modulation[:, 0], ROWS, axis=0)
    scale = jnp.repeat(modulation[:, 1], ROWS, axis=0)
    gate = jnp.repeat(modulation[:, 2], ROWS, axis=0)
    floats = latents.astype(jnp.float32)
    row_mean = lax.optimization_barrier(jnp.mean(floats, axis=1, keepdims=True))
    row_square = lax.optimization_barrier(jnp.mean(floats * floats, axis=1, keepdims=True))
    normed = ((floats - row_mean) * lax.rsqrt(row_square - row_mean * row_mean + EPSILON) * (1.0 + scale) + shift).astype(jnp.bfloat16)
    queries = head_norm(jnp.dot(normed, w_query, preferred_element_type=jnp.float32), query_gain)
    keys_all = head_norm(jnp.dot(normed, w_key, preferred_element_type=jnp.float32), key_gain)
    values_all = jnp.dot(normed, w_value, preferred_element_type=jnp.float32).astype(jnp.bfloat16).reshape(TOKENS, HEADS, HEAD_DIM)
    span_ids = jnp.arange(SPANS, dtype=jnp.int32)
    ranks = span_order
    slot_ids = jnp.arange(TOKENS, dtype=jnp.int32)
    key_span = slot_ids // ROWS
    key_live = slot_ids % ROWS < span_counts[key_span]
    keys_float = keys_all.astype(jnp.float32)
    values_float = values_all.astype(jnp.float32)
    score_factor = 1.0 / HEAD_DIM ** 0.5

    def one_span(span):
        start = (span * ROWS).astype(jnp.int32)
        query_block = lax.dynamic_slice_in_dim(queries, start, ROWS, 0).astype(jnp.float32)
        linked = (block_mask[span][key_span] == 1) | (key_span == span)
        allowed = (ranks[key_span] <= ranks[span]) & linked & key_live
        scores = jnp.einsum('qhd,khd->hqk', query_block, keys_float) * score_factor
        scores = jnp.where(allowed[None, None, :], scores, NEG_FILL)
        top = lax.optimization_barrier(jnp.max(scores, axis=-1, keepdims=True))
        weights = jnp.where(allowed[None, None, :], jnp.exp(scores - top), 0.0)
        total = lax.optimization_barrier(jnp.sum(weights, axis=-1))
        rounded = weights.astype(jnp.bfloat16).astype(jnp.float32)
        summed = jnp.einsum('hqk,khd->qhd', rounded, values_float)
        attended = summed / jnp.transpose(total)[:, :, None]
        return attended.astype(jnp.bfloat16).reshape(ROWS, HEADS * HEAD_DIM)
    attended = lax.map(one_span, span_ids).reshape(TOKENS, HEADS * HEAD_DIM)
    group_width = HEADS * HEAD_DIM // N_TENSOR
    projected = jnp.zeros((TOKENS, D), jnp.float32)
    for group in range(N_TENSOR):
        term = jnp.dot(attended[:, group * group_width:(group + 1) * group_width], w_out[group * group_width:(group + 1) * group_width], preferred_element_type=jnp.float32)
        term = lax.optimization_barrier(term.astype(jnp.bfloat16))
        projected = projected + term.astype(jnp.float32)
    return (floats + gate * projected).astype(jnp.bfloat16)
```

```python
import functools
import math

import jax
import jax.numpy as jnp
from jax import lax
from jax.experimental import pallas as pl
from jax.experimental.pallas import tpu as pltpu
from jax.sharding import Mesh
from jax.sharding import PartitionSpec as P

HEAD_DIM = 128
HEADS_HERE = 3
WIDTH = HEADS_HERE * HEAD_DIM
SIDE = 4
ROWS = 512
HALF = ROWS // 2
EPSILON = 1e-06
NEG_FILL = -1e30
LOG2E = math.log2(math.e)
STEPS = (0, -1, 1, 2)
AXES = ("y", "x", "z", "core")
STAT_ROWS = 16


def permute(value, move):
    pairs = []
    for y in range(SIDE):
        for x in range(SIDE):
            for z in range(SIDE):
                for c in range(2):
                    source = ((y * SIDE + x) * SIDE + z) * 2 + c
                    ty, tx, tz, tc = move(y, x, z, c)
                    target = (((ty % SIDE) * SIDE + tx % SIDE) * SIDE + tz % SIDE) * 2 + tc
                    pairs.append((source, target))
    return lax.ppermute(value, AXES, pairs)


def along_z(step):
    return lambda y, x, z, c: (y, x, z + step, c)


def other_core(y, x, z, c):
    return (y, x, z, 1 - c)


def along_keys(step):
    return lambda y, x, z, c: (y, x + step, z, c) if c == 0 else (y + step, x, z, c)


def along_queries(step):
    return lambda y, x, z, c: (y + step, x, z, c) if c == 0 else (y, x + step, z, c)


def norm_kernel(columns, level, *refs):
    pieces, mod_ref, out_ref = refs[:16], refs[16], refs[17]
    rows = pieces[0].shape[0]
    wide = pieces[0].shape[1]
    block = 16
    for half in range(2):
        here = pieces[half * 8 : half * 8 + 8]

        def chunk(step, carry, here=here, half=half):
            at = pl.ds(pl.multiple_of(step * block, block), block)
            total = jnp.zeros((block, 128), jnp.float32)
            square = jnp.zeros((block, 128), jnp.float32)
            for piece in here:
                value = piece[at, :].astype(jnp.float32)
                for g in range(wide // 128):
                    part = value[:, g * 128 : (g + 1) * 128]
                    total = total + part
                    square = square + part * part
            mean = jnp.sum(total, axis=1, keepdims=True) * (1.0 / (8 * wide))
            mean_square = jnp.sum(square, axis=1, keepdims=True) * (1.0 / (8 * wide))
            factor = lax.rsqrt(mean_square - mean * mean + EPSILON)
            for index, piece in enumerate(here):
                place = pl.ds(pl.multiple_of(columns[index], 128), wide)
                value = piece[at, :].astype(jnp.float32)
                scaled = (value - mean) * factor * (1.0 + mod_ref[0, 1:2, place]) + mod_ref[0, 0:1, place]
                out_ref[half, at, place] = scaled.astype(jnp.bfloat16)
            return carry

        lax.fori_loop(0, rows // block, chunk, 0)


def normalise(pieces, columns, level, mod_table):
    rows, wide = pieces[0].shape
    tile = 64
    total = wide * 8
    grid_spec = pltpu.PrefetchScalarGridSpec(
        num_scalar_prefetch=2,
        grid=(rows // tile,),
        in_specs=[pl.BlockSpec((tile, wide), lambda i, c, l: (i, 0))] * 16
        + [pl.BlockSpec((1, 3, total), lambda i, c, l: (l[0], 0, 0))],
        out_specs=pl.BlockSpec((2, tile, total), lambda i, c, l: (0, i, 0)),
    )
    out = pl.pallas_call(
        norm_kernel,
        grid_spec=grid_spec,
        out_shape=jax.ShapeDtypeStruct((2, rows, total), jnp.bfloat16),
        name="normalise",
    )(columns, level, *pieces, mod_table)
    return out.reshape(2 * rows, total)


def head_norm_kernel(in_ref, gain_ref, out_ref):
    for h in range(HEADS_HERE):
        part = in_ref[:, h * HEAD_DIM : (h + 1) * HEAD_DIM]
        mean = jnp.mean(part * part, axis=1, keepdims=True)
        scaled = part * lax.rsqrt(mean + EPSILON) * gain_ref[h : h + 1, :]
        out_ref[:, h * HEAD_DIM : (h + 1) * HEAD_DIM] = scaled.astype(jnp.bfloat16)


def head_norm(projection, gain):
    return pl.pallas_call(
        head_norm_kernel,
        out_shape=jax.ShapeDtypeStruct(projection.shape, jnp.bfloat16),
        name="head_norm",
    )(projection, gain)


def attention_kernel(allowed, counts, *refs):
    q_in, k_in, v_in = refs[0:5], refs[5:9], refs[9:13]
    outs = refs[13:17]
    q_buf, k_buf, v_buf, top_ref, sum_ref, acc_ref, out_buf, sem, out_sem = refs[17:]
    copies = []
    for i in range(3):
        copies.append((q_in[i], q_buf.at[i]))
    copies.append((q_in[3], q_buf.at[3, pl.ds(0, HALF)]))
    copies.append((q_in[4], q_buf.at[3, pl.ds(HALF, HALF)]))
    for j in range(4):
        copies.append((k_in[j], k_buf.at[j]))
        copies.append((v_in[j], v_buf.at[j]))
    started = [pltpu.make_async_copy(a, b, sem.at[n]) for n, (a, b) in enumerate(copies)]
    for copy in started:
        copy.start()
    for copy in started:
        copy.wait()
    scale = LOG2E / math.sqrt(HEAD_DIM)

    def fold(i, j, tiles):
        live = counts[j]
        depth = tiles * 128
        tail = depth - 128
        rows = lax.broadcasted_iota(jnp.int32, (128, ROWS), 0) + tail
        for h in range(HEADS_HERE):
            cut = slice(h * HEAD_DIM, (h + 1) * HEAD_DIM)
            queries = q_buf[i, :, cut]
            parts = []
            if tail > 0:
                parts.append(
                    lax.dot_general(
                        k_buf[j, :tail, cut], queries, (((1,), (1,)), ((), ())), preferred_element_type=jnp.float32
                    )
                )
            last = lax.dot_general(
                k_buf[j, tail:depth, cut], queries, (((1,), (1,)), ((), ())), preferred_element_type=jnp.float32
            )
            parts.append(jnp.where(rows < live, last, NEG_FILL))
            before = top_ref[h]
            peak = before
            for part in parts:
                peak = jnp.maximum(peak, jnp.max(part, axis=0, keepdims=True))
            shift = peak * scale
            weights = [jnp.exp2(part * scale - shift) for part in parts]
            factor = jnp.exp2(before * scale - shift)
            total = sum_ref[h] * factor
            for weight in weights:
                total = total + jnp.sum(weight, axis=0, keepdims=True)
            narrow = [weight.astype(jnp.bfloat16) for weight in weights]
            joined = narrow[0] if len(narrow) == 1 else jnp.concatenate(narrow, axis=0)
            product = lax.dot_general(
                v_buf[j, cut, :depth], joined, (((1,), (0,)), ((), ())), preferred_element_type=jnp.float32
            )
            acc_ref[h] = acc_ref[h] * factor + product
            top_ref[h] = peak
            sum_ref[h] = total

    def query_span(i, carry):
        for h in range(HEADS_HERE):
            top_ref[h] = jnp.full((1, ROWS), NEG_FILL, jnp.float32)
            sum_ref[h] = jnp.zeros((1, ROWS), jnp.float32)
            acc_ref[h] = jnp.zeros((HEAD_DIM, ROWS), jnp.float32)

        def key_span(j, inner):
            tiles = (counts[j] + 127) // 128
            for n in range(1, 5):

                @pl.when((allowed[i * 4 + j] == 1) & (tiles == n))
                def _(n=n):
                    fold(i, j, n)

            return inner

        lax.fori_loop(0, 4, key_span, 0)
        stats = []
        for h in range(HEADS_HERE):
            total = sum_ref[h]
            some = total > 0.0
            safe = jnp.where(some, total, 1.0)
            out_buf[i, h * HEAD_DIM : (h + 1) * HEAD_DIM, :] = (acc_ref[h] / safe).astype(jnp.bfloat16)
            size = jnp.where(some, top_ref[h] * scale + jnp.log2(safe), NEG_FILL)
            high = size.astype(jnp.bfloat16).astype(jnp.float32)
            middle = (size - high).astype(jnp.bfloat16).astype(jnp.float32)
            stats += [high, middle, size - high - middle]
        stats.append(jnp.zeros((STAT_ROWS - len(stats), ROWS), jnp.float32))
        out_buf[i, WIDTH:, :] = jnp.concatenate(stats, axis=0).astype(jnp.bfloat16)
        return carry

    lax.fori_loop(0, 4, query_span, 0)
    started = [pltpu.make_async_copy(out_buf.at[i], outs[i], out_sem.at[i]) for i in range(4)]
    for copy in started:
        copy.start()
    for copy in started:
        copy.wait()


def attention(allowed, counts, queries, keys, values):
    tall = WIDTH + STAT_ROWS
    return pl.pallas_call(
        attention_kernel,
        in_specs=[pl.BlockSpec(memory_space=pltpu.SMEM)] * 2 + [pl.BlockSpec(memory_space=pl.ANY)] * 13,
        out_specs=[pl.BlockSpec(memory_space=pl.ANY)] * 4,
        out_shape=[jax.ShapeDtypeStruct((tall, ROWS), jnp.bfloat16)] * 4,
        scratch_shapes=[
            pltpu.VMEM((4, ROWS, WIDTH), jnp.bfloat16),
            pltpu.VMEM((4, ROWS, WIDTH), jnp.bfloat16),
            pltpu.VMEM((4, WIDTH, ROWS), jnp.bfloat16),
            pltpu.VMEM((HEADS_HERE, 1, ROWS), jnp.float32),
            pltpu.VMEM((HEADS_HERE, 1, ROWS), jnp.float32),
            pltpu.VMEM((HEADS_HERE, HEAD_DIM, ROWS), jnp.float32),
            pltpu.VMEM((4, tall, ROWS), jnp.bfloat16),
            pltpu.SemaphoreType.DMA((13,)),
            pltpu.SemaphoreType.DMA((4,)),
        ],
        name="attention",
    )(allowed, counts, *queries, *keys, *values)


def combine_kernel(*refs):
    parts, out_ref = refs[:4], refs[4]
    stats = [part[WIDTH:, :].astype(jnp.float32) for part in parts]
    for h in range(HEADS_HERE):
        sizes = [s[3 * h : 3 * h + 1] + s[3 * h + 1 : 3 * h + 2] + s[3 * h + 2 : 3 * h + 3] for s in stats]
        peak = functools.reduce(jnp.maximum, sizes)
        shares = [jnp.exp2(size - peak) for size in sizes]
        total = functools.reduce(jnp.add, shares)
        cut = slice(h * HEAD_DIM, (h + 1) * HEAD_DIM)
        merged = sum(part[cut, :].astype(jnp.float32) * (share / total) for part, share in zip(parts, shares))
        out_ref[cut, :] = merged.astype(jnp.bfloat16)


def combine(parts):
    return pl.pallas_call(
        combine_kernel,
        out_shape=jax.ShapeDtypeStruct((WIDTH, ROWS), jnp.bfloat16),
        name="combine",
    )(*parts)


def on_device(
    latents,
    w_query,
    w_key,
    w_value,
    w_out,
    query_gain,
    key_gain,
    mod_table,
    levels,
    span_counts,
    block_mask,
    span_order,
):
    shard_width = latents.shape[1]
    y, x, z, c = (lax.axis_index(name) for name in AXES)

    mask_rows = jnp.concatenate(
        [
            block_mask,
            permute(block_mask, along_queries(1)),
            permute(block_mask, along_queries(-1)),
            permute(block_mask, along_queries(2)),
        ]
    )

    own = (latents[:HALF], latents[HALF:])
    below = [None, None]
    above = [None, None]
    below[0] = permute(own[0], along_z(1))
    above[1] = permute(own[1], along_z(-1))
    below[1] = permute(own[1], along_z(1))
    above[0] = permute(own[0], along_z(-1))
    far = (permute(below[0], along_z(1)), permute(above[1], along_z(-1)))
    pieces = []
    for half in range(2):
        for value in (own[half], below[half], above[half], far[half]):
            pieces += [value, permute(value, other_core)]
    columns = jnp.stack(
        [((z + step + SIDE) % SIDE * 2 + core) * shard_width for step in STEPS for core in (c, 1 - c)]
    ).astype(jnp.int32)
    normed = normalise(pieces, columns, levels, mod_table)

    key_own = head_norm(jnp.dot(normed, w_key, preferred_element_type=jnp.float32), key_gain)
    value_own = lax.dot_general(
        w_value, normed, (((0,), (1,)), ((), ())), preferred_element_type=jnp.float32
    ).astype(jnp.bfloat16)
    query_own = head_norm(jnp.dot(normed, w_query, preferred_element_type=jnp.float32), query_gain)

    key_low, key_high = permute(key_own, along_keys(1)), permute(key_own, along_keys(-1))
    value_low, value_high = permute(value_own, along_keys(1)), permute(value_own, along_keys(-1))
    query_low, query_high = permute(query_own, along_queries(1)), permute(query_own, along_queries(-1))
    key_far = permute(key_low, along_keys(1))
    value_far = permute(value_high, along_keys(-1))
    query_far = (
        permute(query_low[:HALF], along_queries(1)),
        permute(query_high[HALF:], along_queries(-1)),
    )

    def spans(along_x):
        return jnp.stack(
            [
                jnp.where(along_x, y * SIDE + (x + s + SIDE) % SIDE, (y + s + SIDE) % SIDE * SIDE + x)
                for s in STEPS
            ]
        )

    query_spans = spans(c == 1)
    key_spans = spans(c == 0)
    ids = jnp.arange(SIDE * SIDE, dtype=jnp.int32)
    pick_query = query_spans[:, None] == ids[None, :]
    pick_key = key_spans[:, None] == ids[None, :]
    query_rank = jnp.sum(jnp.where(pick_query, span_order[None, :], 0), axis=1)
    key_rank = jnp.sum(jnp.where(pick_key, span_order[None, :], 0), axis=1)
    counts = jnp.sum(jnp.where(pick_key, span_counts[None, :], 0), axis=1)
    linked = jnp.sum(jnp.where(pick_key[None, :, :], mask_rows[:, None, :], 0), axis=2) == 1
    same = query_spans[:, None] == key_spans[None, :]
    allowed = ((key_rank[None, :] <= query_rank[:, None]) & (linked | same)).astype(jnp.int32).reshape(-1)

    partial = attention(
        allowed,
        counts,
        (query_own, query_low, query_high, *query_far),
        (key_own, key_low, key_high, key_far),
        (value_own, value_low, value_high, value_far),
    )
    attended = combine(
        (
            partial[0],
            permute(partial[1], along_queries(-1)),
            permute(partial[2], along_queries(1)),
            permute(partial[3], along_queries(2)),
        )
    )

    partial_out = lax.dot_general(attended, w_out, (((0,), (0,)), ((), ())), preferred_element_type=jnp.float32)
    projected = lax.psum_scatter(
        partial_out.astype(jnp.bfloat16), ("z", "core"), scatter_dimension=1, tiled=True
    ).astype(jnp.float32)
    gate_row = lax.dynamic_slice(mod_table, (levels[0], 2, (z * 2 + c) * shard_width), (1, 1, shard_width))[0]
    return (latents.astype(jnp.float32) + gate_row * projected).astype(jnp.bfloat16)


def solution(mesh):
    fine = Mesh(mesh.devices.reshape(SIDE, SIDE, SIDE, 2), AXES)
    frame, tensor = ("y", "x"), ("z", "core")
    return jax.shard_map(
        on_device,
        mesh=fine,
        in_specs=(
            P(frame, tensor),
            P(None, tensor),
            P(None, tensor),
            P(None, tensor),
            P(tensor, None),
            P(tensor, None),
            P(tensor, None),
            P(),
            P(frame),
            P(),
            P(frame, None),
            P(),
        ),
        out_specs=P(frame, tensor),
        check_vma=False,
    )
```

```python
import functools
import math

import jax
import jax.numpy as jnp
from jax import lax
from jax.experimental import pallas as pl
from jax.experimental.pallas import tpu as pltpu
from jax.sharding import Mesh
from jax.sharding import PartitionSpec as P


HEAD_DIM = 128
HEADS_HERE = 3
WIDTH = HEADS_HERE * HEAD_DIM
SIDE = 4
ROWS = 512
HALF = ROWS // 2
EPSILON = 1e-06
NEG_FILL = -1e30
LOG2E = math.log2(math.e)
STEPS = (0, -1, 1, 2)
AXES = ("y", "x", "z", "core")
STAT_ROWS = 16


def permute(value, move):
    pairs = []
    for y in range(SIDE):
        for x in range(SIDE):
            for z in range(SIDE):
                for c in range(2):
                    source = ((y * SIDE + x) * SIDE + z) * 2 + c
                    ty, tx, tz, tc = move(y, x, z, c)
                    target = (((ty % SIDE) * SIDE + tx % SIDE) * SIDE + tz % SIDE) * 2 + tc
                    pairs.append((source, target))
    return lax.ppermute(value, AXES, pairs)


def along_z(step):
    return lambda y, x, z, c: (y, x, z + step, c)


def other_core(y, x, z, c):
    return (y, x, z, 1 - c)


def along_keys(step):
    return lambda y, x, z, c: (y, x + step, z, c) if c == 0 else (y + step, x, z, c)


def along_queries(step):
    return lambda y, x, z, c: (y + step, x, z, c) if c == 0 else (y, x + step, z, c)


def in_vmem(value):
    return pltpu.with_memory_space_constraint(value, pltpu.VMEM)


def project_kernel(places, *refs):
    pieces = refs[:16]
    mod_ref, gain_q, gain_k, wq_ref, wk_ref, wv_ref = refs[16:22]
    q_ref, k_ref, v_ref = refs[22:25]
    mean_ref, factor_ref, n_even, n_odd, acc_q, acc_k, acc_v = refs[25:]
    wide = pieces[0].shape[1]
    groups = wide // 128
    block = 64
    for half in range(2):
        here = pieces[half * 8 : half * 8 + 8]

        def chunk(n, carry, here=here, half=half):
            at = pl.ds(pl.multiple_of(n * block, block), block)
            total = jnp.zeros((block, 128), jnp.float32)
            square = jnp.zeros((block, 128), jnp.float32)
            for piece in here:
                for g in range(groups):
                    part = piece[at, g * 128 : (g + 1) * 128].astype(jnp.float32)
                    total = total + part
                    square = square + part * part
            mean = jnp.sum(total, axis=1, keepdims=True) * (1.0 / (8 * wide))
            mean_square = jnp.sum(square, axis=1, keepdims=True) * (1.0 / (8 * wide))
            factor = lax.rsqrt(mean_square - mean * mean + EPSILON)
            to = pl.ds(pl.multiple_of(half * HALF + n * block, block), block)
            mean_ref[to, :] = jnp.broadcast_to(mean, (block, 128))
            factor_ref[to, :] = jnp.broadcast_to(factor, (block, 128))
            return carry

        lax.fori_loop(0, HALF // block, chunk, 0)
    core = places[4]
    for n in range(SIDE):
        n_buf = n_odd if n % 2 else n_even
        start = places[n] * (2 * wide)
        for e in range(2):
            inside = (core if e == 0 else 1 - core) * wide
            at = pl.ds(pl.multiple_of(start + inside, 128), wide)
            shift = mod_ref[0:1, at]
            scale = 1.0 + mod_ref[1:2, at]
            for half in range(2):
                rows = slice(half * HALF, (half + 1) * HALF)
                mean = jnp.concatenate([mean_ref[rows, :]] * groups, axis=1)
                factor = jnp.concatenate([factor_ref[rows, :]] * groups, axis=1)
                value = pieces[half * 8 + 2 * n + e][...].astype(jnp.float32)
                normed = (value - mean) * factor * scale + shift
                n_buf[rows, pl.ds(pl.multiple_of(inside, 128), wide)] = normed.astype(jnp.bfloat16)
        at = pl.ds(pl.multiple_of(start, 128), 2 * wide)
        for acc, weight in ((acc_k, wk_ref), (acc_v, wv_ref), (acc_q, wq_ref)):
            product = lax.dot_general(
                weight[at, :], n_buf[...], (((0,), (1,)), ((), ())), preferred_element_type=jnp.float32
            )
            if n == 0:
                acc[...] = product
            else:
                acc[...] += product
    for acc, gain, out, turn in ((acc_q, gain_q, q_ref, False), (acc_k, gain_k, k_ref, True)):
        for h in range(HEADS_HERE):
            cut = slice(h * HEAD_DIM, (h + 1) * HEAD_DIM)
            part = acc[cut, :]
            square = jnp.mean(part * part, axis=0, keepdims=True)
            gains = jnp.transpose(jnp.broadcast_to(gain[h : h + 1, :], (HEAD_DIM, HEAD_DIM)))
            gains = jnp.concatenate([gains] * (ROWS // HEAD_DIM), axis=1)
            scaled = part * lax.rsqrt(square + EPSILON) * gains
            if turn:
                out[:, cut] = jnp.transpose(scaled).astype(jnp.bfloat16)
            else:
                out[cut, :] = scaled.astype(jnp.bfloat16)
    v_ref[...] = acc_v[...].astype(jnp.bfloat16)


def project(pieces, places, modulation, gains, weights):
    wide = pieces[0].shape[1]
    vmem = pl.BlockSpec(memory_space=pltpu.VMEM)
    operands = [in_vmem(v) for v in (*pieces, modulation, *gains, *weights)]
    return pl.pallas_call(
        project_kernel,
        in_specs=[pl.BlockSpec(memory_space=pltpu.SMEM)] + [vmem] * 22,
        out_specs=[vmem] * 3,
        out_shape=[
            pltpu.VMEM((WIDTH, ROWS), jnp.bfloat16),
            pltpu.VMEM((ROWS, WIDTH), jnp.bfloat16),
            pltpu.VMEM((WIDTH, ROWS), jnp.bfloat16),
        ],
        scratch_shapes=[
            pltpu.VMEM((ROWS, 128), jnp.float32),
            pltpu.VMEM((ROWS, 128), jnp.float32),
            pltpu.VMEM((ROWS, 2 * wide), jnp.bfloat16),
            pltpu.VMEM((ROWS, 2 * wide), jnp.bfloat16),
            pltpu.VMEM((WIDTH, ROWS), jnp.float32),
            pltpu.VMEM((WIDTH, ROWS), jnp.float32),
            pltpu.VMEM((WIDTH, ROWS), jnp.float32),
        ],
        compiler_params=pltpu.CompilerParams(vmem_limit_bytes=24 * 2**20),
        name="project",
    )(places, *operands)


def attention_kernel(allowed, counts, *refs):
    q_in, k_in, v_in = refs[0:5], refs[5:9], refs[9:13]
    outs = refs[13:17]
    q_buf, k_buf, v_buf, top_ref, sum_ref, acc_ref, out_buf, sem, out_sem = refs[17:]
    copies = []
    for i in range(3):
        copies.append((q_in[i], q_buf.at[i]))
    copies.append((q_in[3], q_buf.at[3, pl.ds(0, WIDTH // 2)]))
    copies.append((q_in[4], q_buf.at[3, pl.ds(WIDTH // 2, WIDTH // 2)]))
    for j in range(4):
        copies.append((k_in[j], k_buf.at[j]))
        copies.append((v_in[j], v_buf.at[j]))
    started = [pltpu.make_async_copy(a, b, sem.at[n]) for n, (a, b) in enumerate(copies)]
    for copy in started:
        copy.start()
    for copy in started:
        copy.wait()
    scale = LOG2E / math.sqrt(HEAD_DIM)

    def fold(i, j, tiles):
        live = counts[j]
        depth = tiles * 128
        tail = depth - 128
        rows = lax.broadcasted_iota(jnp.int32, (128, ROWS), 0) + tail
        for h in range(HEADS_HERE):
            cut = slice(h * HEAD_DIM, (h + 1) * HEAD_DIM)
            queries = q_buf[i, cut, :]
            parts = []
            if tail > 0:
                parts.append(
                    lax.dot_general(
                        k_buf[j, :tail, cut], queries, (((1,), (0,)), ((), ())), preferred_element_type=jnp.float32
                    )
                )
            last = lax.dot_general(
                k_buf[j, tail:depth, cut], queries, (((1,), (0,)), ((), ())), preferred_element_type=jnp.float32
            )
            parts.append(jnp.where(rows < live, last, NEG_FILL))
            before = top_ref[h]
            peak = before
            for part in parts:
                peak = jnp.maximum(peak, jnp.max(part, axis=0, keepdims=True))
            shift = peak * scale
            weights = [jnp.exp2(part * scale - shift) for part in parts]
            factor = jnp.exp2(before * scale - shift)
            total = sum_ref[h] * factor
            for weight in weights:
                total = total + jnp.sum(weight, axis=0, keepdims=True)
            narrow = [weight.astype(jnp.bfloat16) for weight in weights]
            joined = narrow[0] if len(narrow) == 1 else jnp.concatenate(narrow, axis=0)
            product = lax.dot_general(
                v_buf[j, cut, :depth], joined, (((1,), (0,)), ((), ())), preferred_element_type=jnp.float32
            )
            acc_ref[h] = acc_ref[h] * factor + product
            top_ref[h] = peak
            sum_ref[h] = total

    def query_span(i, carry):
        for h in range(HEADS_HERE):
            top_ref[h] = jnp.full((1, ROWS), NEG_FILL, jnp.float32)
            sum_ref[h] = jnp.zeros((1, ROWS), jnp.float32)
            acc_ref[h] = jnp.zeros((HEAD_DIM, ROWS), jnp.float32)

        def key_span(j, inner):
            tiles = (counts[j] + 127) // 128
            for n in range(1, 5):

                @pl.when((allowed[i * 4 + j] == 1) & (tiles == n))
                def _(n=n):
                    fold(i, j, n)

            return inner

        lax.fori_loop(0, 4, key_span, 0)
        stats = []
        for h in range(HEADS_HERE):
            total = sum_ref[h]
            some = total > 0.0
            safe = jnp.where(some, total, 1.0)
            out_buf[i, h * HEAD_DIM : (h + 1) * HEAD_DIM, :] = (acc_ref[h] / safe).astype(jnp.bfloat16)
            size = jnp.where(some, top_ref[h] * scale + jnp.log2(safe), NEG_FILL)
            high = size.astype(jnp.bfloat16).astype(jnp.float32)
            middle = (size - high).astype(jnp.bfloat16).astype(jnp.float32)
            stats += [high, middle, size - high - middle]
        stats.append(jnp.zeros((STAT_ROWS - len(stats), ROWS), jnp.float32))
        out_buf[i, WIDTH:, :] = jnp.concatenate(stats, axis=0).astype(jnp.bfloat16)
        return carry

    lax.fori_loop(0, 4, query_span, 0)
    started = [pltpu.make_async_copy(out_buf.at[i], outs[i], out_sem.at[i]) for i in range(4)]
    for copy in started:
        copy.start()
    for copy in started:
        copy.wait()


def attention(allowed, counts, queries, keys, values):
    tall = WIDTH + STAT_ROWS
    return pl.pallas_call(
        attention_kernel,
        in_specs=[pl.BlockSpec(memory_space=pltpu.SMEM)] * 2 + [pl.BlockSpec(memory_space=pl.ANY)] * 13,
        out_specs=[pl.BlockSpec(memory_space=pl.ANY)] * 4,
        out_shape=[jax.ShapeDtypeStruct((tall, ROWS), jnp.bfloat16)] * 4,
        scratch_shapes=[
            pltpu.VMEM((4, WIDTH, ROWS), jnp.bfloat16),
            pltpu.VMEM((4, ROWS, WIDTH), jnp.bfloat16),
            pltpu.VMEM((4, WIDTH, ROWS), jnp.bfloat16),
            pltpu.VMEM((HEADS_HERE, 1, ROWS), jnp.float32),
            pltpu.VMEM((HEADS_HERE, 1, ROWS), jnp.float32),
            pltpu.VMEM((HEADS_HERE, HEAD_DIM, ROWS), jnp.float32),
            pltpu.VMEM((4, tall, ROWS), jnp.bfloat16),
            pltpu.SemaphoreType.DMA((13,)),
            pltpu.SemaphoreType.DMA((4,)),
        ],
        name="attention",
    )(allowed, counts, *queries, *keys, *values)


def combine_kernel(*refs):
    parts, out_ref = refs[:4], refs[4]
    stats = [part[WIDTH:, :].astype(jnp.float32) for part in parts]
    for h in range(HEADS_HERE):
        sizes = [s[3 * h : 3 * h + 1] + s[3 * h + 1 : 3 * h + 2] + s[3 * h + 2 : 3 * h + 3] for s in stats]
        peak = functools.reduce(jnp.maximum, sizes)
        shares = [jnp.exp2(size - peak) for size in sizes]
        total = functools.reduce(jnp.add, shares)
        cut = slice(h * HEAD_DIM, (h + 1) * HEAD_DIM)
        merged = sum(part[cut, :].astype(jnp.float32) * (share / total) for part, share in zip(parts, shares))
        out_ref[:, cut] = jnp.transpose(merged).astype(jnp.bfloat16)


def combine(parts):
    vmem = pl.BlockSpec(memory_space=pltpu.VMEM)
    return pl.pallas_call(
        combine_kernel,
        in_specs=[vmem] * 4,
        out_specs=vmem,
        out_shape=pltpu.VMEM((ROWS, WIDTH), jnp.bfloat16),
        compiler_params=pltpu.CompilerParams(vmem_limit_bytes=16 * 2**20),
        name="combine",
    )(*[in_vmem(part) for part in parts])


def output_kernel(*refs):
    attended, weights = refs[:8], refs[8:12]
    latents_ref, gate_ref, out_ref, acc_ref = refs[12:16]
    for n in range(8):
        term = jnp.dot(attended[n][...], weights[n // 2][n % 2], preferred_element_type=jnp.float32)
        term = term.astype(jnp.bfloat16).astype(jnp.float32)
        if n == 0:
            acc_ref[...] = term
        elif n < 7:
            acc_ref[...] += term
        else:
            projected = acc_ref[...] + term
            updated = latents_ref[...].astype(jnp.float32) + gate_ref[...] * projected
            out_ref[...] = updated.astype(jnp.bfloat16)


def output(attended, weights, latents, gate):
    vmem = pl.BlockSpec(memory_space=pltpu.VMEM)
    wide = latents.shape[1]
    operands = [in_vmem(v) for v in (*attended, *weights, latents, gate)]
    return pl.pallas_call(
        output_kernel,
        in_specs=[vmem] * 14,
        out_specs=vmem,
        out_shape=jax.ShapeDtypeStruct(latents.shape, jnp.bfloat16),
        scratch_shapes=[pltpu.VMEM((ROWS, wide), jnp.float32)],
        compiler_params=pltpu.CompilerParams(vmem_limit_bytes=16 * 2**20),
        name="output",
    )(*operands)


def on_device(
    latents,
    w_query,
    w_key,
    w_value,
    w_out,
    query_gain,
    key_gain,
    mod_table,
    levels,
    span_counts,
    block_mask,
    span_order,
):
    shard_width = latents.shape[1]
    y, x, z, c = (lax.axis_index(name) for name in AXES)

    mask_low = permute(block_mask, along_queries(1))
    mask_high = permute(block_mask, along_queries(-1))
    mask_far = permute(block_mask, along_queries(2))
    mask_rows = jnp.concatenate([block_mask, mask_low, mask_high, mask_far])
    own = (latents[:HALF], latents[HALF:])
    below, above = [None, None], [None, None]
    below[0] = permute(own[0], along_z(1))
    above[1] = permute(own[1], along_z(-1))
    below[1] = permute(own[1], along_z(1))
    above[0] = permute(own[0], along_z(-1))

    places = [(z + step + SIDE) % SIDE * 2 + core for step in STEPS for core in (c, 1 - c)]
    columns = jnp.stack([(z + step + SIDE) % SIDE for step in STEPS] + [c]).astype(jnp.int32)
    modulation = lax.dynamic_index_in_dim(mod_table, levels[0], 0, keepdims=False)
    gate = lax.dynamic_slice(modulation, (2, places[0] * shard_width), (1, shard_width))

    def spans(along_x):
        return jnp.stack(
            [
                jnp.where(along_x, y * SIDE + (x + s + SIDE) % SIDE, (y + s + SIDE) % SIDE * SIDE + x)
                for s in STEPS
            ]
        )

    query_spans = spans(c == 1)
    key_spans = spans(c == 0)
    ids = jnp.arange(SIDE * SIDE, dtype=jnp.int32)
    pick_query = query_spans[:, None] == ids[None, :]
    pick_key = key_spans[:, None] == ids[None, :]
    query_rank = jnp.sum(jnp.where(pick_query, span_order[None, :], 0), axis=1)
    key_rank = jnp.sum(jnp.where(pick_key, span_order[None, :], 0), axis=1)
    counts = jnp.sum(jnp.where(pick_key, span_counts[None, :], 0), axis=1)
    linked = jnp.sum(jnp.where(pick_key[None, :, :], mask_rows[:, None, :], 0), axis=2) == 1
    same = query_spans[:, None] == key_spans[None, :]
    allowed = ((key_rank[None, :] <= query_rank[:, None]) & (linked | same)).astype(jnp.int32).reshape(-1)

    w_parts = [
        lax.dynamic_slice(w_out, (0, place * shard_width), (WIDTH, shard_width)) for place in places
    ]
    w_other = permute(jnp.stack(w_parts[1::2]), other_core)
    w_pairs = [jnp.stack((w_parts[2 * n], w_other[n])) for n in range(SIDE)]
    below[0], allowed, counts, columns, modulation, gate, w_pairs = lax.optimization_barrier(
        (below[0], allowed, counts, columns, modulation, gate, w_pairs)
    )

    far = (permute(below[0], along_z(1)), permute(above[1], along_z(-1)))
    pieces = []
    for half in range(2):
        for value in (own[half], below[half], above[half], far[half]):
            pieces += [value, permute(value, other_core)]
    query_own, key_own, value_own = project(
        pieces, columns, modulation, (query_gain, key_gain), (w_query, w_key, w_value)
    )

    w_pairs, key_own, value_own, query_own = lax.optimization_barrier((w_pairs, key_own, value_own, query_own))
    key_low, key_high = permute(key_own, along_keys(1)), permute(key_own, along_keys(-1))
    value_low, value_high = permute(value_own, along_keys(1)), permute(value_own, along_keys(-1))
    query_low, query_high = permute(query_own, along_queries(1)), permute(query_own, along_queries(-1))
    w_below = permute(w_pairs[2], along_z(1))
    w_above = permute(w_pairs[1], along_z(-1))
    w_far = permute(w_pairs[3], along_z(2))
    w_blocks = (w_pairs[0], w_below, w_above, w_far)
    key_far = permute(key_low, along_keys(1))
    value_far = permute(value_high, along_keys(-1))
    query_far = (
        permute(query_low[: WIDTH // 2], along_queries(1)),
        permute(query_high[WIDTH // 2 :], along_queries(-1)),
    )

    partial = attention(
        allowed,
        counts,
        (query_own, query_low, query_high, *query_far),
        (key_own, key_low, key_high, key_far),
        (value_own, value_low, value_high, value_far),
    )
    attended = combine(
        (
            partial[0],
            permute(partial[1], along_queries(-1)),
            permute(partial[2], along_queries(1)),
            permute(partial[3], along_queries(2)),
        )
    )
    shared = [attended, permute(attended, along_z(1)), permute(attended, along_z(-1)), permute(attended, along_z(2))]
    everyone = []
    for value in shared:
        everyone += [value, permute(value, other_core)]
    return output(everyone, w_blocks, latents, gate)


def solution(mesh):
    fine = Mesh(mesh.devices.reshape(SIDE, SIDE, SIDE, 2), AXES)
    frame, tensor = ("y", "x"), ("z", "core")

    return jax.shard_map(
        on_device,
        mesh=fine,
        in_specs=(
            P(frame, tensor),
            P(None, tensor),
            P(None, tensor),
            P(None, tensor),
            P(tensor, None),
            P(tensor, None),
            P(tensor, None),
            P(),
            P(frame),
            P(),
            P(frame, None),
            P(),
        ),
        out_specs=P(frame, tensor),
        check_vma=False,
    )
```

```python
import functools
import math

import jax
import jax.numpy as jnp
from jax import lax
from jax.experimental import pallas as pl
from jax.experimental.pallas import tpu as pltpu
from jax.sharding import Mesh
from jax.sharding import PartitionSpec as P


HEAD_DIM = 128
HEADS_HERE = 3
WIDTH = HEADS_HERE * HEAD_DIM
SIDE = 4
ROWS = 512
HALF = ROWS // 2
EPSILON = 1e-06
NEG_FILL = -1e30
LOG2E = math.log2(math.e)
STEPS = (0, -1, 1, 2)
AXES = ("y", "x", "z", "core")
STAT_ROWS = 16


def permute(value, move):
    pairs = []
    for y in range(SIDE):
        for x in range(SIDE):
            for z in range(SIDE):
                for c in range(2):
                    source = ((y * SIDE + x) * SIDE + z) * 2 + c
                    ty, tx, tz, tc = move(y, x, z, c)
                    target = (((ty % SIDE) * SIDE + tx % SIDE) * SIDE + tz % SIDE) * 2 + tc
                    pairs.append((source, target))
    return lax.ppermute(value, AXES, pairs)


def along_z(step):
    return lambda y, x, z, c: (y, x, z + step, c)


def other_core(y, x, z, c):
    return (y, x, z, 1 - c)


def along_keys(step):
    return lambda y, x, z, c: (y, x + step, z, c) if c == 0 else (y + step, x, z, c)


def along_queries(step):
    return lambda y, x, z, c: (y + step, x, z, c) if c == 0 else (y, x + step, z, c)


def in_vmem(value):
    return pltpu.with_memory_space_constraint(value, pltpu.VMEM)


def project_kernel(places, *refs):
    pieces = refs[:16]
    mod_ref, gain_q, gain_k, *w_refs = refs[16:22]
    q_ref, k_ref, v_ref = refs[22:25]
    mean_ref, factor_ref, n_even, n_odd, acc_q, acc_k, acc_v, w_buf, sem = refs[25:]
    wide = pieces[0].shape[1]
    w_copies = []
    for n in range(SIDE):
        at = pl.ds(pl.multiple_of(places[n] * (2 * wide), 128), 2 * wide)
        for m in range(3):
            copy = pltpu.make_async_copy(w_refs[m].at[at], w_buf.at[n, m], sem.at[3 * n + m])
            copy.start()
            w_copies.append(copy)
    groups = wide // 128
    block = 64
    for half in range(2):
        here = pieces[half * 8 : half * 8 + 8]

        def chunk(n, carry, here=here, half=half):
            at = pl.ds(pl.multiple_of(n * block, block), block)
            total = jnp.zeros((block, 128), jnp.float32)
            square = jnp.zeros((block, 128), jnp.float32)
            for piece in here:
                for g in range(groups):
                    part = piece[at, g * 128 : (g + 1) * 128].astype(jnp.float32)
                    total = total + part
                    square = square + part * part
            mean = jnp.sum(total, axis=1, keepdims=True) * (1.0 / (8 * wide))
            mean_square = jnp.sum(square, axis=1, keepdims=True) * (1.0 / (8 * wide))
            factor = lax.rsqrt(mean_square - mean * mean + EPSILON)
            to = pl.ds(pl.multiple_of(half * HALF + n * block, block), block)
            mean_ref[to, :] = jnp.broadcast_to(mean, (block, 128))
            factor_ref[to, :] = jnp.broadcast_to(factor, (block, 128))
            return carry

        lax.fori_loop(0, HALF // block, chunk, 0)
    core = places[4]
    for n in range(SIDE):
        n_buf = n_odd if n % 2 else n_even
        start = places[n] * (2 * wide)
        for e in range(2):
            inside = (core if e == 0 else 1 - core) * wide
            at = pl.ds(pl.multiple_of(start + inside, 128), wide)
            shift = mod_ref[0:1, at]
            scale = 1.0 + mod_ref[1:2, at]
            for half in range(2):
                rows = slice(half * HALF, (half + 1) * HALF)
                mean = jnp.concatenate([mean_ref[rows, :]] * groups, axis=1)
                factor = jnp.concatenate([factor_ref[rows, :]] * groups, axis=1)
                value = pieces[half * 8 + 2 * n + e][...].astype(jnp.float32)
                normed = (value - mean) * factor * scale + shift
                n_buf[rows, pl.ds(pl.multiple_of(inside, 128), wide)] = normed.astype(jnp.bfloat16)
        for m, acc in ((0, acc_q), (1, acc_k), (2, acc_v)):
            w_copies[3 * n + m].wait()
            product = lax.dot_general(
                w_buf[n, m], n_buf[...], (((0,), (1,)), ((), ())), preferred_element_type=jnp.float32
            )
            if n == 0:
                acc[...] = product
            else:
                acc[...] += product
    for acc, gain, out, turn in ((acc_q, gain_q, q_ref, False), (acc_k, gain_k, k_ref, True)):
        for h in range(HEADS_HERE):
            cut = slice(h * HEAD_DIM, (h + 1) * HEAD_DIM)
            part = acc[cut, :]
            square = jnp.mean(part * part, axis=0, keepdims=True)
            gains = jnp.transpose(jnp.broadcast_to(gain[h : h + 1, :], (HEAD_DIM, HEAD_DIM)))
            gains = jnp.concatenate([gains] * (ROWS // HEAD_DIM), axis=1)
            scaled = part * lax.rsqrt(square + EPSILON) * gains
            if turn:
                out[:, cut] = jnp.transpose(scaled).astype(jnp.bfloat16)
            else:
                out[cut, :] = scaled.astype(jnp.bfloat16)
    v_ref[...] = acc_v[...].astype(jnp.bfloat16)


def project(pieces, places, modulation, gains, weights):
    wide = pieces[0].shape[1]
    vmem = pl.BlockSpec(memory_space=pltpu.VMEM)
    operands = [in_vmem(v) for v in (*pieces, modulation, *gains)]
    operands += [pltpu.with_memory_space_constraint(v, pltpu.HBM) for v in weights]
    return pl.pallas_call(
        project_kernel,
        in_specs=[pl.BlockSpec(memory_space=pltpu.SMEM)]
        + [vmem] * 19
        + [pl.BlockSpec(memory_space=pltpu.HBM)] * 3,
        out_specs=[vmem] * 3,
        out_shape=[
            pltpu.VMEM((WIDTH, ROWS), jnp.bfloat16),
            pltpu.VMEM((ROWS, WIDTH), jnp.bfloat16),
            pltpu.VMEM((WIDTH, ROWS), jnp.bfloat16),
        ],
        scratch_shapes=[
            pltpu.VMEM((ROWS, 128), jnp.float32),
            pltpu.VMEM((ROWS, 128), jnp.float32),
            pltpu.VMEM((ROWS, 2 * wide), jnp.bfloat16),
            pltpu.VMEM((ROWS, 2 * wide), jnp.bfloat16),
            pltpu.VMEM((WIDTH, ROWS), jnp.float32),
            pltpu.VMEM((WIDTH, ROWS), jnp.float32),
            pltpu.VMEM((WIDTH, ROWS), jnp.float32),
            pltpu.VMEM((SIDE, 3, 2 * wide, WIDTH), jnp.bfloat16),
            pltpu.SemaphoreType.DMA((3 * SIDE,)),
        ],
        compiler_params=pltpu.CompilerParams(vmem_limit_bytes=26 * 2**20),
        name="project",
    )(places, *operands)


GRAIN = 128
FAR_GRAIN = 256
SCALE = LOG2E / math.sqrt(HEAD_DIM)


def fold(queries, keys, values, live, depth, grain, acc_ref, stat_ref, i):
    tail = depth - grain
    rows = lax.broadcasted_iota(jnp.int32, (grain, ROWS), 0) + tail
    for h in range(HEADS_HERE):
        cut = slice(h * HEAD_DIM, (h + 1) * HEAD_DIM)
        query = queries(h)
        parts = []
        if tail > 0:
            parts.append(jnp.dot(keys(slice(0, tail), cut), query, preferred_element_type=jnp.float32))
        last = jnp.dot(keys(slice(tail, depth), cut), query, preferred_element_type=jnp.float32)
        parts.append(jnp.where(rows < live, last, NEG_FILL))
        before = stat_ref[i, h : h + 1, :]
        peak = before
        for part in parts:
            peak = jnp.maximum(peak, jnp.max(part, axis=0, keepdims=True))
        shift = peak * SCALE
        weights = [jnp.exp2(part * SCALE - shift) for part in parts]
        factor = jnp.exp2(before * SCALE - shift)
        total = stat_ref[i, 3 + h : 4 + h, :] * factor
        for weight in weights:
            total = total + jnp.sum(weight, axis=0, keepdims=True)
        narrow = [weight.astype(jnp.bfloat16) for weight in weights]
        joined = narrow[0] if len(narrow) == 1 else jnp.concatenate(narrow, axis=0)
        product = jnp.dot(values(cut, slice(0, depth)), joined, preferred_element_type=jnp.float32)
        acc_ref[i, cut, :] = acc_ref[i, cut, :] * factor + product
        stat_ref[i, h : h + 1, :] = peak
        stat_ref[i, 3 + h : 4 + h, :] = total


def each_size(wanted, live, grain, run):
    for depth in range(grain, ROWS + 1, grain):

        @pl.when((wanted == 1) & (live <= depth) & (live > depth - grain))
        def _(depth=depth):
            run(depth)


def clear(acc_ref, stat_ref, i):
    acc_ref[i] = jnp.zeros((WIDTH, ROWS), jnp.float32)
    stat_ref[i, 0:3, :] = jnp.full((3, ROWS), NEG_FILL, jnp.float32)
    stat_ref[i, 3:8, :] = jnp.zeros((5, ROWS), jnp.float32)


def finish(acc_ref, stat_ref, i, out_ref):
    stats = []
    for h in range(HEADS_HERE):
        cut = slice(h * HEAD_DIM, (h + 1) * HEAD_DIM)
        total = stat_ref[i, 3 + h : 4 + h, :]
        some = total > 0.0
        safe = jnp.where(some, total, 1.0)
        out_ref[cut, :] = (acc_ref[i, cut, :] / safe).astype(jnp.bfloat16)
        size = jnp.where(some, stat_ref[i, h : h + 1, :] * SCALE + jnp.log2(safe), NEG_FILL)
        high = size.astype(jnp.bfloat16).astype(jnp.float32)
        middle = (size - high).astype(jnp.bfloat16).astype(jnp.float32)
        stats += [high, middle, size - high - middle]
    stats.append(jnp.zeros((STAT_ROWS - len(stats), ROWS), jnp.float32))
    out_ref[WIDTH:, :] = jnp.concatenate(stats, axis=0).astype(jnp.bfloat16)


def near_kernel(allowed, counts, *refs):
    q_in, k_in, v_in = refs[0:3], refs[3:6], refs[6:9]
    acc_ref, stat_ref, q_buf, k_buf, v_buf, sem = refs[9:]
    copies = []
    for source, target in ((q_in, q_buf), (k_in, k_buf), (v_in, v_buf)):
        for n in range(3):
            copies.append(pltpu.make_async_copy(source[n], target.at[n], sem.at[len(copies)]))
    for copy in copies:
        copy.start()
    for i in range(3):
        clear(acc_ref, stat_ref, i)

    def pair(n, carry):
        i, j = n // 3, n % 3

        @pl.when(j == 0)
        def _():
            pltpu.make_async_copy(q_in[0], q_buf.at[i], sem.at[i]).wait()

        @pl.when(i == 0)
        def _():
            pltpu.make_async_copy(k_in[0], k_buf.at[j], sem.at[3 + j]).wait()
            pltpu.make_async_copy(v_in[0], v_buf.at[j], sem.at[6 + j]).wait()

        each_size(
            allowed[i * 4 + j],
            counts[j],
            GRAIN,
            lambda depth: fold(
                lambda h: q_buf[i, h * HEAD_DIM : (h + 1) * HEAD_DIM, :],
                lambda rows, cut: k_buf[j, rows, cut],
                lambda cut, rows: v_buf[j, cut, rows],
                counts[j],
                depth,
                GRAIN,
                acc_ref,
                stat_ref,
                i,
            ),
        )
        return carry

    lax.fori_loop(0, 9, pair, 0)


def attend_near(allowed, counts, queries, keys, values):
    vmem = pl.BlockSpec(memory_space=pltpu.VMEM)
    return pl.pallas_call(
        near_kernel,
        in_specs=[pl.BlockSpec(memory_space=pltpu.SMEM)] * 2 + [vmem] * 9,
        out_specs=[vmem] * 2,
        out_shape=[pltpu.VMEM((3, WIDTH, ROWS), jnp.float32), pltpu.VMEM((3, 8, ROWS), jnp.float32)],
        scratch_shapes=[
            pltpu.VMEM((3, WIDTH, ROWS), jnp.bfloat16),
            pltpu.VMEM((3, ROWS, WIDTH), jnp.bfloat16),
            pltpu.VMEM((3, WIDTH, ROWS), jnp.bfloat16),
            pltpu.SemaphoreType.DMA((9,)),
        ],
        compiler_params=pltpu.CompilerParams(vmem_limit_bytes=18 * 2**20),
        name="attend_near",
    )(allowed, counts, *[in_vmem(v) for v in (*queries, *keys, *values)])


def far_kernel(allowed, counts, *refs):
    q_in, k_in, v_in, acc_in, stat_in = refs[0:4], refs[4:8], refs[8:12], refs[12], refs[13]
    outs = refs[14:18]
    q_buf, k_buf, v_buf, acc_ref, stat_ref, sem = refs[18:]
    for n in range(4):
        pltpu.make_async_copy(k_in[n], k_buf.at[n], sem.at[n]).start()
        pltpu.make_async_copy(v_in[n], v_buf.at[n], sem.at[4 + n]).start()
    for n in range(3):
        pltpu.make_async_copy(q_in[n], q_buf.at[n], sem.at[8 + n]).start()
    q_buf[3] = q_in[3][...]
    stat_ref[:3] = stat_in[...]
    clear(acc_ref, stat_ref, 3)

    def block(n, carry):
        i = jnp.where(n < 4, 3, n - 4)
        j = jnp.minimum(n, 3)

        @pl.when(n < 4)
        def _():
            pltpu.make_async_copy(k_in[0], k_buf.at[j], sem.at[j]).wait()
            pltpu.make_async_copy(v_in[0], v_buf.at[j], sem.at[4 + j]).wait()

        @pl.when(n >= 4)
        def _():
            acc_ref[i] = acc_in[i]
            pltpu.make_async_copy(q_in[0], q_buf.at[i], sem.at[8 + i]).wait()

        each_size(
            allowed[i * 4 + j],
            counts[j],
            FAR_GRAIN,
            lambda depth: fold(
                lambda h: q_buf[i, h * HEAD_DIM : (h + 1) * HEAD_DIM, :],
                lambda rows, cut: k_buf[j, rows, cut],
                lambda cut, rows: v_buf[j, cut, rows],
                counts[j],
                depth,
                FAR_GRAIN,
                acc_ref,
                stat_ref,
                i,
            ),
        )
        return carry

    lax.fori_loop(0, 7, block, 0)
    for i in range(4):
        finish(acc_ref, stat_ref, i, outs[i])


def attend_far(allowed, counts, queries, keys, values, state):
    vmem = pl.BlockSpec(memory_space=pltpu.VMEM)
    return pl.pallas_call(
        far_kernel,
        in_specs=[pl.BlockSpec(memory_space=pltpu.SMEM)] * 2 + [vmem] * 14,
        out_specs=[vmem] * 4,
        out_shape=[pltpu.VMEM((WIDTH + STAT_ROWS, ROWS), jnp.bfloat16)] * 4,
        scratch_shapes=[
            pltpu.VMEM((4, WIDTH, ROWS), jnp.bfloat16),
            pltpu.VMEM((4, ROWS, WIDTH), jnp.bfloat16),
            pltpu.VMEM((4, WIDTH, ROWS), jnp.bfloat16),
            pltpu.VMEM((4, WIDTH, ROWS), jnp.float32),
            pltpu.VMEM((4, 8, ROWS), jnp.float32),
            pltpu.SemaphoreType.DMA((11,)),
        ],
        compiler_params=pltpu.CompilerParams(vmem_limit_bytes=22 * 2**20),
        name="attend_far",
    )(allowed, counts, *[in_vmem(v) for v in (*queries, *keys, *values, *state)])


def combine_kernel(*refs):
    parts, out_ref = refs[:4], refs[4]
    stats = [part[WIDTH:, :].astype(jnp.float32) for part in parts]
    for h in range(HEADS_HERE):
        sizes = [s[3 * h : 3 * h + 1] + s[3 * h + 1 : 3 * h + 2] + s[3 * h + 2 : 3 * h + 3] for s in stats]
        peak = functools.reduce(jnp.maximum, sizes)
        shares = [jnp.exp2(size - peak) for size in sizes]
        total = functools.reduce(jnp.add, shares)
        cut = slice(h * HEAD_DIM, (h + 1) * HEAD_DIM)
        merged = sum(part[cut, :].astype(jnp.float32) * (share / total) for part, share in zip(parts, shares))
        out_ref[:, cut] = jnp.transpose(merged).astype(jnp.bfloat16)


def combine(parts):
    vmem = pl.BlockSpec(memory_space=pltpu.VMEM)
    return pl.pallas_call(
        combine_kernel,
        in_specs=[vmem] * 4,
        out_specs=vmem,
        out_shape=pltpu.VMEM((ROWS, WIDTH), jnp.bfloat16),
        compiler_params=pltpu.CompilerParams(vmem_limit_bytes=8 * 2**20),
        name="combine",
    )(*[in_vmem(part) for part in parts])


def head_terms(attended, weights):
    for n, value in enumerate(attended):
        term = jnp.dot(value[...], weights[n // 2][n % 2], preferred_element_type=jnp.float32)
        yield term.astype(jnp.bfloat16).astype(jnp.float32)


def output_own_kernel(first_ref, second_ref, weight_ref, acc_ref):
    first, second = head_terms((first_ref, second_ref), (weight_ref,))
    acc_ref[...] = first + second


def output_rest_kernel(acc_in, *refs):
    attended, weights, latents_ref, gate_ref, out_ref, acc_ref = refs[:6], refs[6:9], *refs[9:]
    acc_ref[...] = acc_in[...]
    for n, term in enumerate(head_terms(attended, weights)):
        if n < 5:
            acc_ref[...] += term
        else:
            projected = acc_ref[...] + term
            updated = latents_ref[...].astype(jnp.float32) + gate_ref[...] * projected
            out_ref[...] = updated.astype(jnp.bfloat16)


def output_own(attended, weight):
    vmem = pl.BlockSpec(memory_space=pltpu.VMEM)
    return pl.pallas_call(
        output_own_kernel,
        in_specs=[vmem] * 3,
        out_specs=vmem,
        out_shape=pltpu.VMEM((ROWS, weight.shape[2]), jnp.float32),
        compiler_params=pltpu.CompilerParams(vmem_limit_bytes=10 * 2**20),
        name="output_own",
    )(*[in_vmem(v) for v in (*attended, weight)])


def output_rest(acc, attended, weights, latents, gate):
    vmem = pl.BlockSpec(memory_space=pltpu.VMEM)
    return pl.pallas_call(
        output_rest_kernel,
        in_specs=[vmem] * 12,
        out_specs=vmem,
        out_shape=jax.ShapeDtypeStruct(latents.shape, jnp.bfloat16),
        scratch_shapes=[pltpu.VMEM(latents.shape, jnp.float32)],
        compiler_params=pltpu.CompilerParams(vmem_limit_bytes=12 * 2**20),
        name="output_rest",
    )(*[in_vmem(v) for v in (acc, *attended, *weights, latents, gate)])


def take_kernel(places, w_ref, out_ref, sem):
    wide = out_ref.shape[2]
    copies = []
    for n in range(SIDE):
        columns = pl.ds(pl.multiple_of(places[2 * n + 1] * wide, 128), wide)
        copies.append(pltpu.make_async_copy(w_ref.at[:, columns], out_ref.at[n], sem.at[n]))
    for copy in copies:
        copy.start()
    for copy in copies:
        copy.wait()


def take_other(places, w_out, wide):
    return pl.pallas_call(
        take_kernel,
        in_specs=[pl.BlockSpec(memory_space=pltpu.SMEM), pl.BlockSpec(memory_space=pltpu.HBM)],
        out_specs=pl.BlockSpec(memory_space=pltpu.VMEM),
        out_shape=pltpu.VMEM((SIDE, WIDTH, wide), jnp.bfloat16),
        scratch_shapes=[pltpu.SemaphoreType.DMA((SIDE,))],
        compiler_params=pltpu.CompilerParams(vmem_limit_bytes=8 * 2**20),
        name="take_other",
    )(places, pltpu.with_memory_space_constraint(w_out, pltpu.HBM))


def pair_kernel(places, w_ref, other_ref, *refs):
    outs, (held, in_sem, own_sem, other_sem) = refs[:SIDE], refs[SIDE:]
    wide = other_ref.shape[2]
    arriving, leaving = [], []
    for n in range(SIDE):
        columns = pl.ds(pl.multiple_of(places[2 * n] * wide, 128), wide)
        arriving.append(pltpu.make_async_copy(w_ref.at[:, columns], held.at[n], in_sem.at[n]))
        arriving[n].start()
    for n in range(SIDE):
        leaving.append(pltpu.make_async_copy(other_ref.at[n], outs[n].at[1], other_sem.at[n]))
        leaving[n].start()
    for n in range(SIDE):
        arriving[n].wait()
        leaving.append(pltpu.make_async_copy(held.at[n], outs[n].at[0], own_sem.at[n]))
        leaving[SIDE + n].start()
    for copy in leaving:
        copy.wait()


def pair_up(places, w_out, w_other):
    hbm = pl.BlockSpec(memory_space=pltpu.HBM)
    return pl.pallas_call(
        pair_kernel,
        in_specs=[pl.BlockSpec(memory_space=pltpu.SMEM), hbm, pl.BlockSpec(memory_space=pltpu.VMEM)],
        out_specs=[hbm] * SIDE,
        out_shape=[pltpu.HBM((2, *w_other.shape[1:]), jnp.bfloat16)] * SIDE,
        scratch_shapes=[
            pltpu.VMEM(w_other.shape, jnp.bfloat16),
            pltpu.SemaphoreType.DMA((SIDE,)),
            pltpu.SemaphoreType.DMA((SIDE,)),
            pltpu.SemaphoreType.DMA((SIDE,)),
        ],
        compiler_params=pltpu.CompilerParams(vmem_limit_bytes=8 * 2**20),
        name="pair_up",
    )(places, pltpu.with_memory_space_constraint(w_out, pltpu.HBM), in_vmem(w_other))


def on_device(
    latents,
    w_query,
    w_key,
    w_value,
    w_out,
    query_gain,
    key_gain,
    mod_table,
    levels,
    span_counts,
    block_mask,
    span_order,
):
    shard_width = latents.shape[1]
    y, x, z, c = (lax.axis_index(name) for name in AXES)

    mask_low = permute(block_mask, along_queries(1))
    mask_high = permute(block_mask, along_queries(-1))
    mask_far = permute(block_mask, along_queries(2))
    mask_rows = jnp.concatenate([block_mask, mask_low, mask_high, mask_far])
    own = (latents[:HALF], latents[HALF:])
    below, above = [None, None], [None, None]
    below[0] = permute(own[0], along_z(1))
    above[1] = permute(own[1], along_z(-1))
    below[1] = permute(own[1], along_z(1))
    above[0] = permute(own[0], along_z(-1))

    places = [(z + step + SIDE) % SIDE * 2 + core for step in STEPS for core in (c, 1 - c)]
    columns = jnp.stack([(z + step + SIDE) % SIDE for step in STEPS] + [c]).astype(jnp.int32)
    modulation = lax.dynamic_index_in_dim(mod_table, levels[0], 0, keepdims=False)
    gate = lax.dynamic_slice(modulation, (2, places[0] * shard_width), (1, shard_width))

    def spans(along_x):
        return jnp.stack(
            [
                jnp.where(along_x, y * SIDE + (x + s + SIDE) % SIDE, (y + s + SIDE) % SIDE * SIDE + x)
                for s in STEPS
            ]
        )

    query_spans = spans(c == 1)
    key_spans = spans(c == 0)
    ids = jnp.arange(SIDE * SIDE, dtype=jnp.int32)
    pick_query = query_spans[:, None] == ids[None, :]
    pick_key = key_spans[:, None] == ids[None, :]
    query_rank = jnp.sum(jnp.where(pick_query, span_order[None, :], 0), axis=1)
    key_rank = jnp.sum(jnp.where(pick_key, span_order[None, :], 0), axis=1)
    counts = jnp.sum(jnp.where(pick_key, span_counts[None, :], 0), axis=1)
    w_places = jnp.stack(places).astype(jnp.int32)
    w_other = permute(take_other(w_places, w_out, shard_width), other_core)
    w_pairs = pair_up(w_places, w_out, w_other)

    far_low = permute(below[0], along_z(1))
    far_high = permute(above[1], along_z(-1))
    far_low, far_high, columns, modulation, w_pairs, mask_rows = lax.optimization_barrier(
        (far_low, far_high, columns, modulation, w_pairs, mask_rows)
    )
    far = (far_low, far_high)
    linked = jnp.sum(jnp.where(pick_key[None, :, :], mask_rows[:, None, :], 0), axis=2) == 1
    same = query_spans[:, None] == key_spans[None, :]
    allowed = ((key_rank[None, :] <= query_rank[:, None]) & (linked | same)).astype(jnp.int32).reshape(-1)
    pieces = []
    for half in range(2):
        for value in (own[half], below[half], above[half], far[half]):
            pieces += [value, permute(value, other_core)]
    w_below = permute(w_pairs[2], along_z(1))
    w_above = permute(w_pairs[1], along_z(-1))
    w_far = permute(w_pairs[3], along_z(2))
    query_own, key_own, value_own = project(
        pieces, columns, modulation, (query_gain, key_gain), (w_query, w_key, w_value)
    )

    key_low, key_high = permute(key_own, along_keys(1)), permute(key_own, along_keys(-1))
    value_low, value_high = permute(value_own, along_keys(1)), permute(value_own, along_keys(-1))
    query_low, query_high = permute(query_own, along_queries(1)), permute(query_own, along_queries(-1))
    w_blocks = (w_pairs[0], w_below, w_above, w_far)
    key_far = permute(key_low, along_keys(1))
    value_far = permute(value_high, along_keys(-1))
    query_far = permute(query_own, along_queries(2))

    near_queries = (query_own, query_low, query_high)
    near_keys = (key_own, key_low, key_high)
    near_values = (value_own, value_low, value_high)
    state = attend_near(allowed, counts, near_queries, near_keys, near_values)
    partial = attend_far(
        allowed,
        counts,
        (*near_queries, query_far),
        (*near_keys, key_far),
        (*near_values, value_far),
        state,
    )
    sent_far = permute(partial[3], along_queries(2))
    sent_low = permute(partial[1], along_queries(-1))
    sent_high = permute(partial[2], along_queries(1))
    attended = combine((partial[0], sent_low, sent_high, sent_far))

    shared_low = permute(attended, along_z(1))
    shared_high = permute(attended, along_z(-1))
    shared_far = permute(attended, along_z(2))
    own_other = permute(attended, other_core)
    low_other = permute(shared_low, other_core)
    high_other = permute(shared_high, other_core)
    acc = output_own((attended, own_other), w_blocks[0])
    rest = (shared_low, low_other, shared_high, high_other, shared_far, permute(shared_far, other_core))
    return output_rest(acc, rest, w_blocks[1:], latents, gate)


def solution(mesh):
    fine = Mesh(mesh.devices.reshape(SIDE, SIDE, SIDE, 2), AXES)
    frame, tensor = ("y", "x"), ("z", "core")

    return jax.shard_map(
        on_device,
        mesh=fine,
        in_specs=(
            P(frame, tensor),
            P(None, tensor),
            P(None, tensor),
            P(None, tensor),
            P(tensor, None),
            P(tensor, None),
            P(tensor, None),
            P(),
            P(frame),
            P(),
            P(frame, None),
            P(),
        ),
        out_specs=P(frame, tensor),
        check_vma=False,
    )
```

```python
import functools
import math

import jax
import jax.numpy as jnp
from jax import lax
from jax.experimental import pallas as pl
from jax.experimental.pallas import tpu as pltpu
from jax.sharding import Mesh
from jax.sharding import PartitionSpec as P


HEAD_DIM = 128
HEADS_HERE = 3
WIDTH = HEADS_HERE * HEAD_DIM
SIDE = 4
ROWS = 512
HALF = ROWS // 2
EPSILON = 1e-06
NEG_FILL = -1e30
LOG2E = math.log2(math.e)
STEPS = (0, -1, 1, 2)
AXES = ("y", "x", "z", "core")
STAT_ROWS = 16


def permute(value, move):
    pairs = []
    for y in range(SIDE):
        for x in range(SIDE):
            for z in range(SIDE):
                for c in range(2):
                    source = ((y * SIDE + x) * SIDE + z) * 2 + c
                    ty, tx, tz, tc = move(y, x, z, c)
                    target = (((ty % SIDE) * SIDE + tx % SIDE) * SIDE + tz % SIDE) * 2 + tc
                    pairs.append((source, target))
    return lax.ppermute(value, AXES, pairs)


def along_z(step):
    return lambda y, x, z, c: (y, x, z + step, c)


def other_core(y, x, z, c):
    return (y, x, z, 1 - c)


def along_keys(step):
    return lambda y, x, z, c: (y, x + step, z, c) if c == 0 else (y + step, x, z, c)


def along_queries(step):
    return lambda y, x, z, c: (y + step, x, z, c) if c == 0 else (y, x + step, z, c)


def in_vmem(value):
    return pltpu.with_memory_space_constraint(value, pltpu.VMEM)


def project_kernel(places, *refs):
    pieces = refs[:16]
    mod_ref, gain_q, gain_k, *w_refs = refs[16:22]
    q_ref, k_ref, v_ref = refs[22:25]
    mean_ref, factor_ref, n_even, n_odd, acc_q, acc_k, acc_v, w_buf, sem = refs[25:]
    wide = pieces[0].shape[1]
    w_copies = []
    for n in range(SIDE):
        at = pl.ds(pl.multiple_of(places[n] * (2 * wide), 128), 2 * wide)
        for m in range(3):
            copy = pltpu.make_async_copy(w_refs[m].at[at], w_buf.at[n, m], sem.at[3 * n + m])
            copy.start()
            w_copies.append(copy)
    groups = wide // 128
    block = 64
    for half in range(2):
        here = pieces[half * 8 : half * 8 + 8]

        def chunk(n, carry, here=here, half=half):
            at = pl.ds(pl.multiple_of(n * block, block), block)
            total = jnp.zeros((block, 128), jnp.float32)
            square = jnp.zeros((block, 128), jnp.float32)
            for piece in here:
                for g in range(groups):
                    part = piece[at, g * 128 : (g + 1) * 128].astype(jnp.float32)
                    total = total + part
                    square = square + part * part
            mean = jnp.sum(total, axis=1, keepdims=True) * (1.0 / (8 * wide))
            mean_square = jnp.sum(square, axis=1, keepdims=True) * (1.0 / (8 * wide))
            factor = lax.rsqrt(mean_square - mean * mean + EPSILON)
            to = pl.ds(pl.multiple_of(half * HALF + n * block, block), block)
            mean_ref[to, :] = jnp.broadcast_to(mean, (block, 128))
            factor_ref[to, :] = jnp.broadcast_to(factor, (block, 128))
            return carry

        lax.fori_loop(0, HALF // block, chunk, 0)
    core = places[4]
    for n in range(SIDE):
        n_buf = n_odd if n % 2 else n_even
        start = places[n] * (2 * wide)
        for e in range(2):
            inside = (core if e == 0 else 1 - core) * wide
            at = pl.ds(pl.multiple_of(start + inside, 128), wide)
            shift = mod_ref[0:1, at]
            scale = 1.0 + mod_ref[1:2, at]
            for half in range(2):
                rows = slice(half * HALF, (half + 1) * HALF)
                mean = jnp.concatenate([mean_ref[rows, :]] * groups, axis=1)
                factor = jnp.concatenate([factor_ref[rows, :]] * groups, axis=1)
                value = pieces[half * 8 + 2 * n + e][...].astype(jnp.float32)
                normed = (value - mean) * factor * scale + shift
                n_buf[rows, pl.ds(pl.multiple_of(inside, 128), wide)] = normed.astype(jnp.bfloat16)
        for m, acc in ((0, acc_q), (1, acc_k), (2, acc_v)):
            w_copies[3 * n + m].wait()
            product = lax.dot_general(
                w_buf[n, m], n_buf[...], (((0,), (1,)), ((), ())), preferred_element_type=jnp.float32
            )
            if n == 0:
                acc[...] = product
            else:
                acc[...] += product
    for acc, gain, out, turn in ((acc_q, gain_q, q_ref, False), (acc_k, gain_k, k_ref, True)):
        for h in range(HEADS_HERE):
            cut = slice(h * HEAD_DIM, (h + 1) * HEAD_DIM)
            part = acc[cut, :]
            square = jnp.mean(part * part, axis=0, keepdims=True)
            gains = jnp.transpose(jnp.broadcast_to(gain[h : h + 1, :], (HEAD_DIM, HEAD_DIM)))
            gains = jnp.concatenate([gains] * (ROWS // HEAD_DIM), axis=1)
            scaled = part * lax.rsqrt(square + EPSILON) * gains
            if turn:
                out[:, cut] = jnp.transpose(scaled).astype(jnp.bfloat16)
            else:
                out[cut, :] = scaled.astype(jnp.bfloat16)
    v_ref[...] = acc_v[...].astype(jnp.bfloat16)


def project(pieces, places, modulation, gains, weights):
    wide = pieces[0].shape[1]
    vmem = pl.BlockSpec(memory_space=pltpu.VMEM)
    operands = [in_vmem(v) for v in (*pieces, modulation, *gains)]
    operands += [pltpu.with_memory_space_constraint(v, pltpu.HBM) for v in weights]
    return pl.pallas_call(
        project_kernel,
        in_specs=[pl.BlockSpec(memory_space=pltpu.SMEM)]
        + [vmem] * 19
        + [pl.BlockSpec(memory_space=pltpu.HBM)] * 3,
        out_specs=[vmem] * 3,
        out_shape=[
            pltpu.VMEM((WIDTH, ROWS), jnp.bfloat16),
            pltpu.VMEM((ROWS, WIDTH), jnp.bfloat16),
            pltpu.VMEM((WIDTH, ROWS), jnp.bfloat16),
        ],
        scratch_shapes=[
            pltpu.VMEM((ROWS, 128), jnp.float32),
            pltpu.VMEM((ROWS, 128), jnp.float32),
            pltpu.VMEM((ROWS, 2 * wide), jnp.bfloat16),
            pltpu.VMEM((ROWS, 2 * wide), jnp.bfloat16),
            pltpu.VMEM((WIDTH, ROWS), jnp.float32),
            pltpu.VMEM((WIDTH, ROWS), jnp.float32),
            pltpu.VMEM((WIDTH, ROWS), jnp.float32),
            pltpu.VMEM((SIDE, 3, 2 * wide, WIDTH), jnp.bfloat16),
            pltpu.SemaphoreType.DMA((3 * SIDE,)),
        ],
        compiler_params=pltpu.CompilerParams(vmem_limit_bytes=26 * 2**20),
        name="project",
    )(places, *operands)


GRAIN = 128
FAR_GRAIN = 128
SCALE = LOG2E / math.sqrt(HEAD_DIM)


def fold(queries, keys, values, live, depth, grain, acc_ref, stat_ref, i):
    tail = depth - grain
    rows = lax.broadcasted_iota(jnp.int32, (grain, ROWS), 0) + tail
    cuts = [slice(h * HEAD_DIM, (h + 1) * HEAD_DIM) for h in range(HEADS_HERE)]
    scores = []
    for h, cut in enumerate(cuts):
        query = queries(h)
        parts = []
        if tail > 0:
            parts.append(jnp.dot(keys(slice(0, tail), cut), query, preferred_element_type=jnp.float32))
        last = jnp.dot(keys(slice(tail, depth), cut), query, preferred_element_type=jnp.float32)
        parts.append(jnp.where(rows < live, last, NEG_FILL))
        scores.append(parts)
    joined, factors = [], []
    for h, parts in enumerate(scores):
        before = stat_ref[i, h : h + 1, :]
        peak = before
        for part in parts:
            peak = jnp.maximum(peak, jnp.max(part, axis=0, keepdims=True))
        shift = peak * SCALE
        weights = [jnp.exp2(part * SCALE - shift) for part in parts]
        factor = jnp.exp2(before * SCALE - shift)
        total = stat_ref[i, 3 + h : 4 + h, :] * factor
        for weight in weights:
            total = total + jnp.sum(weight, axis=0, keepdims=True)
        narrow = [weight.astype(jnp.bfloat16) for weight in weights]
        joined.append(narrow[0] if len(narrow) == 1 else jnp.concatenate(narrow, axis=0))
        factors.append(factor)
        stat_ref[i, h : h + 1, :] = peak
        stat_ref[i, 3 + h : 4 + h, :] = total
    for h, cut in enumerate(cuts):
        product = jnp.dot(values(cut, slice(0, depth)), joined[h], preferred_element_type=jnp.float32)
        acc_ref[i, cut, :] = acc_ref[i, cut, :] * factors[h] + product


def each_size(wanted, live, grain, run):
    for depth in range(grain, ROWS + 1, grain):

        @pl.when((wanted == 1) & (live <= depth) & (live > depth - grain))
        def _(depth=depth):
            run(depth)


def clear(acc_ref, stat_ref, i):
    acc_ref[i] = jnp.zeros((WIDTH, ROWS), jnp.float32)
    stat_ref[i, 0:3, :] = jnp.full((3, ROWS), NEG_FILL, jnp.float32)
    stat_ref[i, 3:8, :] = jnp.zeros((5, ROWS), jnp.float32)


def finish(acc_ref, stat_ref, i, out_ref):
    stats = []
    for h in range(HEADS_HERE):
        cut = slice(h * HEAD_DIM, (h + 1) * HEAD_DIM)
        total = stat_ref[i, 3 + h : 4 + h, :]
        some = total > 0.0
        safe = jnp.where(some, total, 1.0)
        out_ref[cut, :] = (acc_ref[i, cut, :] / safe).astype(jnp.bfloat16)
        size = jnp.where(some, stat_ref[i, h : h + 1, :] * SCALE + jnp.log2(safe), NEG_FILL)
        high = size.astype(jnp.bfloat16).astype(jnp.float32)
        middle = (size - high).astype(jnp.bfloat16).astype(jnp.float32)
        stats += [high, middle, size - high - middle]
    stats.append(jnp.zeros((STAT_ROWS - len(stats), ROWS), jnp.float32))
    out_ref[WIDTH:, :] = jnp.concatenate(stats, axis=0).astype(jnp.bfloat16)


def near_kernel(allowed, counts, *refs):
    q_in, k_in, v_in = refs[0:3], refs[3:6], refs[6:9]
    acc_ref, stat_ref, q_buf, k_buf, v_buf, sem = refs[9:]
    copies = []
    for source, target in ((q_in, q_buf), (k_in, k_buf), (v_in, v_buf)):
        for n in range(3):
            copies.append(pltpu.make_async_copy(source[n], target.at[n], sem.at[len(copies)]))
    for copy in copies:
        copy.start()
    for i in range(3):
        clear(acc_ref, stat_ref, i)

    def pair(n, carry):
        i, j = n // 3, n % 3

        @pl.when(j == 0)
        def _():
            pltpu.make_async_copy(q_in[0], q_buf.at[i], sem.at[i]).wait()

        @pl.when(i == 0)
        def _():
            pltpu.make_async_copy(k_in[0], k_buf.at[j], sem.at[3 + j]).wait()
            pltpu.make_async_copy(v_in[0], v_buf.at[j], sem.at[6 + j]).wait()

        each_size(
            allowed[i * 4 + j],
            counts[j],
            GRAIN,
            lambda depth: fold(
                lambda h: q_buf[i, h * HEAD_DIM : (h + 1) * HEAD_DIM, :],
                lambda rows, cut: k_buf[j, rows, cut],
                lambda cut, rows: v_buf[j, cut, rows],
                counts[j],
                depth,
                GRAIN,
                acc_ref,
                stat_ref,
                i,
            ),
        )
        return carry

    lax.fori_loop(0, 9, pair, 0)


def attend_near(allowed, counts, queries, keys, values):
    vmem = pl.BlockSpec(memory_space=pltpu.VMEM)
    return pl.pallas_call(
        near_kernel,
        in_specs=[pl.BlockSpec(memory_space=pltpu.SMEM)] * 2 + [vmem] * 9,
        out_specs=[vmem] * 2,
        out_shape=[pltpu.VMEM((3, WIDTH, ROWS), jnp.float32), pltpu.VMEM((3, 8, ROWS), jnp.float32)],
        scratch_shapes=[
            pltpu.VMEM((3, WIDTH, ROWS), jnp.bfloat16),
            pltpu.VMEM((3, ROWS, WIDTH), jnp.bfloat16),
            pltpu.VMEM((3, WIDTH, ROWS), jnp.bfloat16),
            pltpu.SemaphoreType.DMA((9,)),
        ],
        compiler_params=pltpu.CompilerParams(vmem_limit_bytes=18 * 2**20),
        name="attend_near",
    )(allowed, counts, *[in_vmem(v) for v in (*queries, *keys, *values)])


def far_kernel(allowed, counts, *refs):
    q_in, k_in, v_in, acc_in, stat_in = refs[0:4], refs[4:8], refs[8:12], refs[12], refs[13]
    outs = refs[14:18]
    q_buf, k_buf, v_buf, acc_ref, stat_ref, sem = refs[18:]
    for n in range(4):
        pltpu.make_async_copy(k_in[n], k_buf.at[n], sem.at[n]).start()
        pltpu.make_async_copy(v_in[n], v_buf.at[n], sem.at[4 + n]).start()
    for n in range(3):
        pltpu.make_async_copy(q_in[n], q_buf.at[n], sem.at[8 + n]).start()
    q_buf[3] = q_in[3][...]
    stat_ref[:3] = stat_in[...]
    clear(acc_ref, stat_ref, 3)

    def block(n, carry):
        i = jnp.where(n < 4, 3, n - 4)
        j = jnp.minimum(n, 3)

        @pl.when(n < 4)
        def _():
            pltpu.make_async_copy(k_in[0], k_buf.at[j], sem.at[j]).wait()
            pltpu.make_async_copy(v_in[0], v_buf.at[j], sem.at[4 + j]).wait()

        @pl.when(n >= 4)
        def _():
            acc_ref[i] = acc_in[i]
            pltpu.make_async_copy(q_in[0], q_buf.at[i], sem.at[8 + i]).wait()

        each_size(
            allowed[i * 4 + j],
            counts[j],
            FAR_GRAIN,
            lambda depth: fold(
                lambda h: q_buf[i, h * HEAD_DIM : (h + 1) * HEAD_DIM, :],
                lambda rows, cut: k_buf[j, rows, cut],
                lambda cut, rows: v_buf[j, cut, rows],
                counts[j],
                depth,
                FAR_GRAIN,
                acc_ref,
                stat_ref,
                i,
            ),
        )
        return carry

    lax.fori_loop(0, 7, block, 0)
    for i in range(4):
        finish(acc_ref, stat_ref, i, outs[i])


def attend_far(allowed, counts, queries, keys, values, state):
    vmem = pl.BlockSpec(memory_space=pltpu.VMEM)
    return pl.pallas_call(
        far_kernel,
        in_specs=[pl.BlockSpec(memory_space=pltpu.SMEM)] * 2 + [vmem] * 14,
        out_specs=[vmem] * 4,
        out_shape=[pltpu.VMEM((WIDTH + STAT_ROWS, ROWS), jnp.bfloat16)] * 4,
        scratch_shapes=[
            pltpu.VMEM((4, WIDTH, ROWS), jnp.bfloat16),
            pltpu.VMEM((4, ROWS, WIDTH), jnp.bfloat16),
            pltpu.VMEM((4, WIDTH, ROWS), jnp.bfloat16),
            pltpu.VMEM((4, WIDTH, ROWS), jnp.float32),
            pltpu.VMEM((4, 8, ROWS), jnp.float32),
            pltpu.SemaphoreType.DMA((11,)),
        ],
        compiler_params=pltpu.CompilerParams(vmem_limit_bytes=22 * 2**20),
        name="attend_far",
    )(allowed, counts, *[in_vmem(v) for v in (*queries, *keys, *values, *state)])


def combine_kernel(*refs):
    parts, out_ref = refs[:4], refs[4]
    stats = [part[WIDTH:, :].astype(jnp.float32) for part in parts]
    for h in range(HEADS_HERE):
        sizes = [s[3 * h : 3 * h + 1] + s[3 * h + 1 : 3 * h + 2] + s[3 * h + 2 : 3 * h + 3] for s in stats]
        peak = functools.reduce(jnp.maximum, sizes)
        shares = [jnp.exp2(size - peak) for size in sizes]
        total = functools.reduce(jnp.add, shares)
        cut = slice(h * HEAD_DIM, (h + 1) * HEAD_DIM)
        merged = sum(part[cut, :].astype(jnp.float32) * (share / total) for part, share in zip(parts, shares))
        out_ref[:, cut] = jnp.transpose(merged).astype(jnp.bfloat16)


def combine(parts):
    vmem = pl.BlockSpec(memory_space=pltpu.VMEM)
    return pl.pallas_call(
        combine_kernel,
        in_specs=[vmem] * 4,
        out_specs=vmem,
        out_shape=pltpu.VMEM((ROWS, WIDTH), jnp.bfloat16),
        compiler_params=pltpu.CompilerParams(vmem_limit_bytes=8 * 2**20),
        name="combine",
    )(*[in_vmem(part) for part in parts])


def head_terms(attended, weights):
    for n, value in enumerate(attended):
        term = jnp.dot(value[...], weights[n // 2][n % 2], preferred_element_type=jnp.float32)
        yield term.astype(jnp.bfloat16).astype(jnp.float32)


def output_own_kernel(first_ref, second_ref, weight_ref, acc_ref):
    first, second = head_terms((first_ref, second_ref), (weight_ref,))
    acc_ref[...] = first + second


def output_rest_kernel(acc_in, *refs):
    attended, weights, latents_ref, gate_ref, out_ref, acc_ref = refs[:6], refs[6:9], *refs[9:]
    acc_ref[...] = acc_in[...]
    for n, term in enumerate(head_terms(attended, weights)):
        if n < 5:
            acc_ref[...] += term
        else:
            projected = acc_ref[...] + term
            updated = latents_ref[...].astype(jnp.float32) + gate_ref[...] * projected
            out_ref[...] = updated.astype(jnp.bfloat16)


def output_own(attended, weight):
    vmem = pl.BlockSpec(memory_space=pltpu.VMEM)
    return pl.pallas_call(
        output_own_kernel,
        in_specs=[vmem] * 3,
        out_specs=vmem,
        out_shape=pltpu.VMEM((ROWS, weight.shape[2]), jnp.float32),
        compiler_params=pltpu.CompilerParams(vmem_limit_bytes=10 * 2**20),
        name="output_own",
    )(*[in_vmem(v) for v in (*attended, weight)])


def output_rest(acc, attended, weights, latents, gate):
    vmem = pl.BlockSpec(memory_space=pltpu.VMEM)
    return pl.pallas_call(
        output_rest_kernel,
        in_specs=[vmem] * 12,
        out_specs=vmem,
        out_shape=jax.ShapeDtypeStruct(latents.shape, jnp.bfloat16),
        scratch_shapes=[pltpu.VMEM(latents.shape, jnp.float32)],
        compiler_params=pltpu.CompilerParams(vmem_limit_bytes=12 * 2**20),
        name="output_rest",
    )(*[in_vmem(v) for v in (acc, *attended, *weights, latents, gate)])


def take_kernel(places, w_ref, out_ref, sem):
    wide = out_ref.shape[2]
    copies = []
    for n in range(SIDE):
        columns = pl.ds(pl.multiple_of(places[2 * n + 1] * wide, 128), wide)
        copies.append(pltpu.make_async_copy(w_ref.at[:, columns], out_ref.at[n], sem.at[n]))
    for copy in copies:
        copy.start()
    for copy in copies:
        copy.wait()


def take_other(places, w_out, wide):
    return pl.pallas_call(
        take_kernel,
        in_specs=[pl.BlockSpec(memory_space=pltpu.SMEM), pl.BlockSpec(memory_space=pltpu.HBM)],
        out_specs=pl.BlockSpec(memory_space=pltpu.VMEM),
        out_shape=pltpu.VMEM((SIDE, WIDTH, wide), jnp.bfloat16),
        scratch_shapes=[pltpu.SemaphoreType.DMA((SIDE,))],
        compiler_params=pltpu.CompilerParams(vmem_limit_bytes=8 * 2**20),
        name="take_other",
    )(places, pltpu.with_memory_space_constraint(w_out, pltpu.HBM))


def pair_kernel(places, w_ref, other_ref, *refs):
    outs, (held, in_sem, own_sem, other_sem) = refs[:SIDE], refs[SIDE:]
    wide = other_ref.shape[2]
    arriving, leaving = [], []
    for n in range(SIDE):
        columns = pl.ds(pl.multiple_of(places[2 * n] * wide, 128), wide)
        arriving.append(pltpu.make_async_copy(w_ref.at[:, columns], held.at[n], in_sem.at[n]))
        arriving[n].start()
    for n in range(SIDE):
        leaving.append(pltpu.make_async_copy(other_ref.at[n], outs[n].at[1], other_sem.at[n]))
        leaving[n].start()
    for n in range(SIDE):
        arriving[n].wait()
        leaving.append(pltpu.make_async_copy(held.at[n], outs[n].at[0], own_sem.at[n]))
        leaving[SIDE + n].start()
    for copy in leaving:
        copy.wait()


def pair_up(places, w_out, w_other):
    hbm = pl.BlockSpec(memory_space=pltpu.HBM)
    return pl.pallas_call(
        pair_kernel,
        in_specs=[pl.BlockSpec(memory_space=pltpu.SMEM), hbm, pl.BlockSpec(memory_space=pltpu.VMEM)],
        out_specs=[hbm] * SIDE,
        out_shape=[pltpu.HBM((2, *w_other.shape[1:]), jnp.bfloat16)] * SIDE,
        scratch_shapes=[
            pltpu.VMEM(w_other.shape, jnp.bfloat16),
            pltpu.SemaphoreType.DMA((SIDE,)),
            pltpu.SemaphoreType.DMA((SIDE,)),
            pltpu.SemaphoreType.DMA((SIDE,)),
        ],
        compiler_params=pltpu.CompilerParams(vmem_limit_bytes=8 * 2**20),
        name="pair_up",
    )(places, pltpu.with_memory_space_constraint(w_out, pltpu.HBM), in_vmem(w_other))


def on_device(
    latents,
    w_query,
    w_key,
    w_value,
    w_out,
    query_gain,
    key_gain,
    mod_table,
    levels,
    span_counts,
    block_mask,
    span_order,
):
    shard_width = latents.shape[1]
    y, x, z, c = (lax.axis_index(name) for name in AXES)

    mask_low = permute(block_mask, along_queries(1))
    mask_high = permute(block_mask, along_queries(-1))
    mask_far = permute(block_mask, along_queries(2))
    mask_rows = jnp.concatenate([block_mask, mask_low, mask_high, mask_far])
    own = (latents[:HALF], latents[HALF:])
    below, above = [None, None], [None, None]
    below[0] = permute(own[0], along_z(1))
    above[1] = permute(own[1], along_z(-1))
    below[1] = permute(own[1], along_z(1))
    above[0] = permute(own[0], along_z(-1))

    places = [(z + step + SIDE) % SIDE * 2 + core for step in STEPS for core in (c, 1 - c)]
    columns = jnp.stack([(z + step + SIDE) % SIDE for step in STEPS] + [c]).astype(jnp.int32)
    modulation = lax.dynamic_index_in_dim(mod_table, levels[0], 0, keepdims=False)
    gate = lax.dynamic_slice(modulation, (2, places[0] * shard_width), (1, shard_width))

    def spans(along_x):
        return jnp.stack(
            [
                jnp.where(along_x, y * SIDE + (x + s + SIDE) % SIDE, (y + s + SIDE) % SIDE * SIDE + x)
                for s in STEPS
            ]
        )

    query_spans = spans(c == 1)
    key_spans = spans(c == 0)
    ids = jnp.arange(SIDE * SIDE, dtype=jnp.int32)
    pick_query = query_spans[:, None] == ids[None, :]
    pick_key = key_spans[:, None] == ids[None, :]
    query_rank = jnp.sum(jnp.where(pick_query, span_order[None, :], 0), axis=1)
    key_rank = jnp.sum(jnp.where(pick_key, span_order[None, :], 0), axis=1)
    counts = jnp.sum(jnp.where(pick_key, span_counts[None, :], 0), axis=1)
    w_places = jnp.stack(places).astype(jnp.int32)
    w_other = permute(take_other(w_places, w_out, shard_width), other_core)
    w_pairs = pair_up(w_places, w_out, w_other)

    far_low = permute(below[0], along_z(1))
    far_high = permute(above[1], along_z(-1))
    far_low, far_high, columns, modulation, w_pairs, mask_rows = lax.optimization_barrier(
        (far_low, far_high, columns, modulation, w_pairs, mask_rows)
    )
    far = (far_low, far_high)
    linked = jnp.sum(jnp.where(pick_key[None, :, :], mask_rows[:, None, :], 0), axis=2) == 1
    same = query_spans[:, None] == key_spans[None, :]
    allowed = ((key_rank[None, :] <= query_rank[:, None]) & (linked | same)).astype(jnp.int32).reshape(-1)
    pieces = []
    for half in range(2):
        for value in (own[half], below[half], above[half], far[half]):
            pieces += [value, permute(value, other_core)]
    w_below = permute(w_pairs[2], along_z(1))
    w_above = permute(w_pairs[1], along_z(-1))
    w_far = permute(w_pairs[3], along_z(2))
    query_own, key_own, value_own = project(
        pieces, columns, modulation, (query_gain, key_gain), (w_query, w_key, w_value)
    )

    key_low, key_high = permute(key_own, along_keys(1)), permute(key_own, along_keys(-1))
    value_low, value_high = permute(value_own, along_keys(1)), permute(value_own, along_keys(-1))
    query_low, query_high = permute(query_own, along_queries(1)), permute(query_own, along_queries(-1))
    w_blocks = (w_pairs[0], w_below, w_above, w_far)
    key_far = permute(key_low, along_keys(1))
    value_far = permute(value_high, along_keys(-1))
    query_far = permute(query_own, along_queries(2))

    near_queries = (query_own, query_low, query_high)
    near_keys = (key_own, key_low, key_high)
    near_values = (value_own, value_low, value_high)
    state = attend_near(allowed, counts, near_queries, near_keys, near_values)
    partial = attend_far(
        allowed,
        counts,
        (*near_queries, query_far),
        (*near_keys, key_far),
        (*near_values, value_far),
        state,
    )
    sent_far = permute(partial[3], along_queries(2))
    sent_low = permute(partial[1], along_queries(-1))
    sent_high = permute(partial[2], along_queries(1))
    attended = combine((partial[0], sent_low, sent_high, sent_far))

    shared_low = permute(attended, along_z(1))
    shared_high = permute(attended, along_z(-1))
    shared_far = permute(attended, along_z(2))
    own_other = permute(attended, other_core)
    low_other = permute(shared_low, other_core)
    high_other = permute(shared_high, other_core)
    acc = output_own((attended, own_other), w_blocks[0])
    rest = (shared_low, low_other, shared_high, high_other, shared_far, permute(shared_far, other_core))
    return output_rest(acc, rest, w_blocks[1:], latents, gate)


def solution(mesh):
    fine = Mesh(mesh.devices.reshape(SIDE, SIDE, SIDE, 2), AXES)
    frame, tensor = ("y", "x"), ("z", "core")

    return jax.shard_map(
        on_device,
        mesh=fine,
        in_specs=(
            P(frame, tensor),
            P(None, tensor),
            P(None, tensor),
            P(None, tensor),
            P(tensor, None),
            P(tensor, None),
            P(tensor, None),
            P(),
            P(frame),
            P(),
            P(frame, None),
            P(),
        ),
        out_specs=P(frame, tensor),
        check_vma=False,
    )
```

```python
import functools
import math

import jax
import jax.numpy as jnp
from jax import lax
from jax.experimental import pallas as pl
from jax.experimental.pallas import tpu as pltpu
from jax.sharding import Mesh
from jax.sharding import PartitionSpec as P


HEAD_DIM = 128
HEADS_HERE = 3
WIDTH = HEADS_HERE * HEAD_DIM
SIDE = 4
ROWS = 512
HALF = ROWS // 2
EPSILON = 1e-06
NEG_FILL = -1e30
LOG2E = math.log2(math.e)
STEPS = (0, -1, 1, 2)
AXES = ("y", "x", "z", "core")
STAT_ROWS = 16


def permute(value, move):
    pairs = []
    for y in range(SIDE):
        for x in range(SIDE):
            for z in range(SIDE):
                for c in range(2):
                    source = ((y * SIDE + x) * SIDE + z) * 2 + c
                    ty, tx, tz, tc = move(y, x, z, c)
                    target = (((ty % SIDE) * SIDE + tx % SIDE) * SIDE + tz % SIDE) * 2 + tc
                    pairs.append((source, target))
    return lax.ppermute(value, AXES, pairs)


def along_z(step):
    return lambda y, x, z, c: (y, x, z + step, c)


def other_core(y, x, z, c):
    return (y, x, z, 1 - c)


def along_keys(step):
    return lambda y, x, z, c: (y, x + step, z, c) if c == 0 else (y + step, x, z, c)


def along_queries(step):
    return lambda y, x, z, c: (y + step, x, z, c) if c == 0 else (y, x + step, z, c)


def in_vmem(value):
    return pltpu.with_memory_space_constraint(value, pltpu.VMEM)


def project_kernel(places, *refs):
    pieces = refs[:16]
    mod_ref, gain_q, gain_k, *w_refs = refs[16:22]
    q_ref, k_ref, v_ref = refs[22:25]
    mean_ref, factor_ref, n_even, n_odd, acc_q, acc_k, acc_v, w_buf, sem = refs[25:]
    wide = pieces[0].shape[1]
    w_copies = []
    for n in range(SIDE):
        at = pl.ds(pl.multiple_of(places[n] * (2 * wide), 128), 2 * wide)
        for m in range(3):
            copy = pltpu.make_async_copy(w_refs[m].at[at], w_buf.at[n, m], sem.at[3 * n + m])
            copy.start()
            w_copies.append(copy)
    groups = wide // 128
    block = 64
    for half in range(2):
        here = pieces[half * 8 : half * 8 + 8]

        def chunk(n, carry, here=here, half=half):
            at = pl.ds(pl.multiple_of(n * block, block), block)
            total = jnp.zeros((block, 128), jnp.float32)
            square = jnp.zeros((block, 128), jnp.float32)
            for piece in here:
                for g in range(groups):
                    part = piece[at, g * 128 : (g + 1) * 128].astype(jnp.float32)
                    total = total + part
                    square = square + part * part
            mean = jnp.sum(total, axis=1, keepdims=True) * (1.0 / (8 * wide))
            mean_square = jnp.sum(square, axis=1, keepdims=True) * (1.0 / (8 * wide))
            factor = lax.rsqrt(mean_square - mean * mean + EPSILON)
            to = pl.ds(pl.multiple_of(half * HALF + n * block, block), block)
            mean_ref[to, :] = jnp.broadcast_to(mean, (block, 128))
            factor_ref[to, :] = jnp.broadcast_to(factor, (block, 128))
            return carry

        lax.fori_loop(0, HALF // block, chunk, 0)
    core = places[4]
    for n in range(SIDE):
        n_buf = n_odd if n % 2 else n_even
        start = places[n] * (2 * wide)
        for e in range(2):
            inside = (core if e == 0 else 1 - core) * wide
            at = pl.ds(pl.multiple_of(start + inside, 128), wide)
            shift = mod_ref[0:1, at]
            scale = 1.0 + mod_ref[1:2, at]
            for half in range(2):
                rows = slice(half * HALF, (half + 1) * HALF)
                mean = jnp.concatenate([mean_ref[rows, :]] * groups, axis=1)
                factor = jnp.concatenate([factor_ref[rows, :]] * groups, axis=1)
                value = pieces[half * 8 + 2 * n + e][...].astype(jnp.float32)
                normed = (value - mean) * factor * scale + shift
                n_buf[rows, pl.ds(pl.multiple_of(inside, 128), wide)] = normed.astype(jnp.bfloat16)
        for m, acc in ((0, acc_q), (1, acc_k), (2, acc_v)):
            w_copies[3 * n + m].wait()
            product = lax.dot_general(
                w_buf[n, m], n_buf[...], (((0,), (1,)), ((), ())), preferred_element_type=jnp.float32
            )
            if n == 0:
                acc[...] = product
            else:
                acc[...] += product
    for acc, gain, out, turn in ((acc_q, gain_q, q_ref, False), (acc_k, gain_k, k_ref, True)):
        for h in range(HEADS_HERE):
            cut = slice(h * HEAD_DIM, (h + 1) * HEAD_DIM)
            part = acc[cut, :]
            square = jnp.mean(part * part, axis=0, keepdims=True)
            gains = jnp.transpose(jnp.broadcast_to(gain[h : h + 1, :], (HEAD_DIM, HEAD_DIM)))
            gains = jnp.concatenate([gains] * (ROWS // HEAD_DIM), axis=1)
            scaled = part * lax.rsqrt(square + EPSILON) * gains
            if turn:
                out[:, cut] = jnp.transpose(scaled).astype(jnp.bfloat16)
            else:
                out[cut, :] = scaled.astype(jnp.bfloat16)
    v_ref[...] = acc_v[...].astype(jnp.bfloat16)


def project(pieces, places, modulation, gains, weights):
    wide = pieces[0].shape[1]
    vmem = pl.BlockSpec(memory_space=pltpu.VMEM)
    operands = [in_vmem(v) for v in (*pieces, modulation, *gains)]
    operands += [pltpu.with_memory_space_constraint(v, pltpu.HBM) for v in weights]
    return pl.pallas_call(
        project_kernel,
        in_specs=[pl.BlockSpec(memory_space=pltpu.SMEM)]
        + [vmem] * 19
        + [pl.BlockSpec(memory_space=pltpu.HBM)] * 3,
        out_specs=[vmem] * 3,
        out_shape=[
            pltpu.VMEM((WIDTH, ROWS), jnp.bfloat16),
            pltpu.VMEM((ROWS, WIDTH), jnp.bfloat16),
            pltpu.VMEM((WIDTH, ROWS), jnp.bfloat16),
        ],
        scratch_shapes=[
            pltpu.VMEM((ROWS, 128), jnp.float32),
            pltpu.VMEM((ROWS, 128), jnp.float32),
            pltpu.VMEM((ROWS, 2 * wide), jnp.bfloat16),
            pltpu.VMEM((ROWS, 2 * wide), jnp.bfloat16),
            pltpu.VMEM((WIDTH, ROWS), jnp.float32),
            pltpu.VMEM((WIDTH, ROWS), jnp.float32),
            pltpu.VMEM((WIDTH, ROWS), jnp.float32),
            pltpu.VMEM((SIDE, 3, 2 * wide, WIDTH), jnp.bfloat16),
            pltpu.SemaphoreType.DMA((3 * SIDE,)),
        ],
        compiler_params=pltpu.CompilerParams(vmem_limit_bytes=26 * 2**20),
        name="project",
    )(places, *operands)


GRAIN = 128
FAR_GRAIN = 128
SCALE = LOG2E / math.sqrt(HEAD_DIM)


def fold(queries, keys, values, live, depth, grain, acc_ref, stat_ref, i):
    tail = depth - grain
    rows = lax.broadcasted_iota(jnp.int32, (grain, ROWS), 0) + tail
    cuts = [slice(h * HEAD_DIM, (h + 1) * HEAD_DIM) for h in range(HEADS_HERE)]
    scores = []
    for h, cut in enumerate(cuts):
        query = queries(h)
        parts = []
        if tail > 0:
            parts.append(jnp.dot(keys(slice(0, tail), cut), query, preferred_element_type=jnp.float32))
        last = jnp.dot(keys(slice(tail, depth), cut), query, preferred_element_type=jnp.float32)
        parts.append(jnp.where(rows < live, last, NEG_FILL))
        scores.append(parts)
    joined, factors = [], []
    for h, parts in enumerate(scores):
        before = stat_ref[i, h : h + 1, :]
        peak = before
        for part in parts:
            peak = jnp.maximum(peak, jnp.max(part, axis=0, keepdims=True))
        shift = peak * SCALE
        weights = [jnp.exp2(part * SCALE - shift) for part in parts]
        factor = jnp.exp2(before * SCALE - shift)
        total = stat_ref[i, 3 + h : 4 + h, :] * factor
        for weight in weights:
            total = total + jnp.sum(weight, axis=0, keepdims=True)
        narrow = [weight.astype(jnp.bfloat16) for weight in weights]
        joined.append(narrow[0] if len(narrow) == 1 else jnp.concatenate(narrow, axis=0))
        factors.append(factor)
        stat_ref[i, h : h + 1, :] = peak
        stat_ref[i, 3 + h : 4 + h, :] = total
    for h, cut in enumerate(cuts):
        product = jnp.dot(values(cut, slice(0, depth)), joined[h], preferred_element_type=jnp.float32)
        acc_ref[i, cut, :] = acc_ref[i, cut, :] * factors[h] + product


def each_size(wanted, live, grain, run):
    for depth in range(grain, ROWS + 1, grain):

        @pl.when((wanted == 1) & (live <= depth) & (live > depth - grain))
        def _(depth=depth):
            run(depth)


def clear(acc_ref, stat_ref, i):
    acc_ref[i] = jnp.zeros((WIDTH, ROWS), jnp.float32)
    stat_ref[i, 0:3, :] = jnp.full((3, ROWS), NEG_FILL, jnp.float32)
    stat_ref[i, 3:8, :] = jnp.zeros((5, ROWS), jnp.float32)


def finish(acc_ref, stat_ref, i, out_ref):
    stats = []
    for h in range(HEADS_HERE):
        cut = slice(h * HEAD_DIM, (h + 1) * HEAD_DIM)
        total = stat_ref[i, 3 + h : 4 + h, :]
        some = total > 0.0
        safe = jnp.where(some, total, 1.0)
        out_ref[cut, :] = (acc_ref[i, cut, :] / safe).astype(jnp.bfloat16)
        size = jnp.where(some, stat_ref[i, h : h + 1, :] * SCALE + jnp.log2(safe), NEG_FILL)
        high = size.astype(jnp.bfloat16).astype(jnp.float32)
        middle = (size - high).astype(jnp.bfloat16).astype(jnp.float32)
        stats += [high, middle, size - high - middle]
    stats.append(jnp.zeros((STAT_ROWS - len(stats), ROWS), jnp.float32))
    out_ref[WIDTH:, :] = jnp.concatenate(stats, axis=0).astype(jnp.bfloat16)


def near_kernel(allowed, counts, *refs):
    q_in, k_in, v_in = refs[0:3], refs[3:6], refs[6:9]
    acc_ref, stat_ref, q_buf, k_buf, v_buf, sem = refs[9:]
    copies = []
    for source, target in ((q_in, q_buf), (k_in, k_buf), (v_in, v_buf)):
        for n in range(3):
            copies.append(pltpu.make_async_copy(source[n], target.at[n], sem.at[len(copies)]))
    for copy in copies:
        copy.start()
    for i in range(3):
        clear(acc_ref, stat_ref, i)

    def pair(n, carry):
        i, j = n // 3, n % 3

        @pl.when(j == 0)
        def _():
            pltpu.make_async_copy(q_in[0], q_buf.at[i], sem.at[i]).wait()

        @pl.when(i == 0)
        def _():
            pltpu.make_async_copy(k_in[0], k_buf.at[j], sem.at[3 + j]).wait()
            pltpu.make_async_copy(v_in[0], v_buf.at[j], sem.at[6 + j]).wait()

        each_size(
            allowed[i * 4 + j],
            counts[j],
            GRAIN,
            lambda depth: fold(
                lambda h: q_buf[i, h * HEAD_DIM : (h + 1) * HEAD_DIM, :],
                lambda rows, cut: k_buf[j, rows, cut],
                lambda cut, rows: v_buf[j, cut, rows],
                counts[j],
                depth,
                GRAIN,
                acc_ref,
                stat_ref,
                i,
            ),
        )
        return carry

    lax.fori_loop(0, 9, pair, 0)


def attend_near(allowed, counts, queries, keys, values):
    vmem = pl.BlockSpec(memory_space=pltpu.VMEM)
    return pl.pallas_call(
        near_kernel,
        in_specs=[pl.BlockSpec(memory_space=pltpu.SMEM)] * 2 + [vmem] * 9,
        out_specs=[vmem] * 2,
        out_shape=[pltpu.VMEM((3, WIDTH, ROWS), jnp.float32), pltpu.VMEM((3, 8, ROWS), jnp.float32)],
        scratch_shapes=[
            pltpu.VMEM((3, WIDTH, ROWS), jnp.bfloat16),
            pltpu.VMEM((3, ROWS, WIDTH), jnp.bfloat16),
            pltpu.VMEM((3, WIDTH, ROWS), jnp.bfloat16),
            pltpu.SemaphoreType.DMA((9,)),
        ],
        compiler_params=pltpu.CompilerParams(vmem_limit_bytes=18 * 2**20),
        name="attend_near",
    )(allowed, counts, *[in_vmem(v) for v in (*queries, *keys, *values)])


def far_kernel(allowed, counts, *refs):
    q_in, k_in, v_in, acc_in, stat_in = refs[0:4], refs[4:8], refs[8:12], refs[12], refs[13]
    outs = refs[14:18]
    q_buf, k_buf, v_buf, acc_ref, stat_ref, sem = refs[18:]
    for n in range(4):
        pltpu.make_async_copy(k_in[n], k_buf.at[n], sem.at[n]).start()
        pltpu.make_async_copy(v_in[n], v_buf.at[n], sem.at[4 + n]).start()
    for n in range(3):
        pltpu.make_async_copy(q_in[n], q_buf.at[n], sem.at[8 + n]).start()
    q_buf[3] = q_in[3][...]
    stat_ref[:3] = stat_in[...]
    clear(acc_ref, stat_ref, 3)

    def block(n, carry):
        i = jnp.where(n < 4, 3, n - 4)
        j = jnp.minimum(n, 3)

        @pl.when(n < 4)
        def _():
            pltpu.make_async_copy(k_in[0], k_buf.at[j], sem.at[j]).wait()
            pltpu.make_async_copy(v_in[0], v_buf.at[j], sem.at[4 + j]).wait()

        @pl.when(n >= 4)
        def _():
            acc_ref[i] = acc_in[i]
            pltpu.make_async_copy(q_in[0], q_buf.at[i], sem.at[8 + i]).wait()

        each_size(
            allowed[i * 4 + j],
            counts[j],
            FAR_GRAIN,
            lambda depth: fold(
                lambda h: q_buf[i, h * HEAD_DIM : (h + 1) * HEAD_DIM, :],
                lambda rows, cut: k_buf[j, rows, cut],
                lambda cut, rows: v_buf[j, cut, rows],
                counts[j],
                depth,
                FAR_GRAIN,
                acc_ref,
                stat_ref,
                i,
            ),
        )
        return carry

    lax.fori_loop(0, 7, block, 0)
    for i in range(4):
        finish(acc_ref, stat_ref, i, outs[i])


def attend_far(allowed, counts, queries, keys, values, state):
    vmem = pl.BlockSpec(memory_space=pltpu.VMEM)
    return pl.pallas_call(
        far_kernel,
        in_specs=[pl.BlockSpec(memory_space=pltpu.SMEM)] * 2 + [vmem] * 14,
        out_specs=[vmem] * 4,
        out_shape=[pltpu.VMEM((WIDTH + STAT_ROWS, ROWS), jnp.bfloat16)] * 4,
        scratch_shapes=[
            pltpu.VMEM((4, WIDTH, ROWS), jnp.bfloat16),
            pltpu.VMEM((4, ROWS, WIDTH), jnp.bfloat16),
            pltpu.VMEM((4, WIDTH, ROWS), jnp.bfloat16),
            pltpu.VMEM((4, WIDTH, ROWS), jnp.float32),
            pltpu.VMEM((4, 8, ROWS), jnp.float32),
            pltpu.SemaphoreType.DMA((11,)),
        ],
        compiler_params=pltpu.CompilerParams(vmem_limit_bytes=22 * 2**20),
        name="attend_far",
    )(allowed, counts, *[in_vmem(v) for v in (*queries, *keys, *values, *state)])


def combine_kernel(*refs):
    parts, out_ref = refs[:4], refs[4]
    stats = [part[WIDTH:, :].astype(jnp.float32) for part in parts]
    for h in range(HEADS_HERE):
        sizes = [s[3 * h : 3 * h + 1] + s[3 * h + 1 : 3 * h + 2] + s[3 * h + 2 : 3 * h + 3] for s in stats]
        peak = functools.reduce(jnp.maximum, sizes)
        shares = [jnp.exp2(size - peak) for size in sizes]
        total = functools.reduce(jnp.add, shares)
        cut = slice(h * HEAD_DIM, (h + 1) * HEAD_DIM)
        merged = sum(part[cut, :].astype(jnp.float32) * (share / total) for part, share in zip(parts, shares))
        out_ref[:, cut] = jnp.transpose(merged).astype(jnp.bfloat16)


def combine(parts):
    vmem = pl.BlockSpec(memory_space=pltpu.VMEM)
    return pl.pallas_call(
        combine_kernel,
        in_specs=[vmem] * 4,
        out_specs=vmem,
        out_shape=pltpu.VMEM((ROWS, WIDTH), jnp.bfloat16),
        compiler_params=pltpu.CompilerParams(vmem_limit_bytes=8 * 2**20),
        name="combine",
    )(*[in_vmem(part) for part in parts])


def group_terms(first, second, weight):
    both = jnp.concatenate([first[...], second[...]], axis=1)
    depth, wide = 2 * weight.shape[1], weight.shape[2]
    return jnp.dot(both, weight[...].reshape(depth, wide), preferred_element_type=jnp.float32)


def output_own_kernel(first_ref, second_ref, weight_ref, acc_ref):
    acc_ref[...] = group_terms(first_ref, second_ref, weight_ref)


def output_rest_kernel(acc_in, *refs):
    attended, weights, latents_ref, gate_ref, out_ref = refs[:6], refs[6:9], *refs[9:]
    projected = acc_in[...]
    for n in range(3):
        projected = projected + group_terms(attended[2 * n], attended[2 * n + 1], weights[n])
    updated = latents_ref[...].astype(jnp.float32) + gate_ref[...] * projected
    out_ref[...] = updated.astype(jnp.bfloat16)


def output_own(attended, weight):
    vmem = pl.BlockSpec(memory_space=pltpu.VMEM)
    return pl.pallas_call(
        output_own_kernel,
        in_specs=[vmem] * 3,
        out_specs=vmem,
        out_shape=pltpu.VMEM((ROWS, weight.shape[2]), jnp.float32),
        compiler_params=pltpu.CompilerParams(vmem_limit_bytes=10 * 2**20),
        name="output_own",
    )(*[in_vmem(v) for v in (*attended, weight)])


def output_rest(acc, attended, weights, latents, gate):
    vmem = pl.BlockSpec(memory_space=pltpu.VMEM)
    return pl.pallas_call(
        output_rest_kernel,
        in_specs=[vmem] * 12,
        out_specs=vmem,
        out_shape=jax.ShapeDtypeStruct(latents.shape, jnp.bfloat16),
        compiler_params=pltpu.CompilerParams(vmem_limit_bytes=12 * 2**20),
        name="output_rest",
    )(*[in_vmem(v) for v in (acc, *attended, *weights, latents, gate)])


def take_kernel(places, w_ref, out_ref, sem):
    wide = out_ref.shape[2]
    copies = []
    for n in range(SIDE):
        columns = pl.ds(pl.multiple_of(places[2 * n + 1] * wide, 128), wide)
        copies.append(pltpu.make_async_copy(w_ref.at[:, columns], out_ref.at[n], sem.at[n]))
    for copy in copies:
        copy.start()
    for copy in copies:
        copy.wait()


def take_other(places, w_out, wide):
    return pl.pallas_call(
        take_kernel,
        in_specs=[pl.BlockSpec(memory_space=pltpu.SMEM), pl.BlockSpec(memory_space=pltpu.HBM)],
        out_specs=pl.BlockSpec(memory_space=pltpu.VMEM),
        out_shape=pltpu.VMEM((SIDE, WIDTH, wide), jnp.bfloat16),
        scratch_shapes=[pltpu.SemaphoreType.DMA((SIDE,))],
        compiler_params=pltpu.CompilerParams(vmem_limit_bytes=8 * 2**20),
        name="take_other",
    )(places, pltpu.with_memory_space_constraint(w_out, pltpu.HBM))


def pair_kernel(places, w_ref, other_ref, *refs):
    outs, (held, in_sem, own_sem, other_sem) = refs[:SIDE], refs[SIDE:]
    wide = other_ref.shape[2]
    arriving, leaving = [], []
    for n in range(SIDE):
        columns = pl.ds(pl.multiple_of(places[2 * n] * wide, 128), wide)
        arriving.append(pltpu.make_async_copy(w_ref.at[:, columns], held.at[n], in_sem.at[n]))
        arriving[n].start()
    for n in range(SIDE):
        leaving.append(pltpu.make_async_copy(other_ref.at[n], outs[n].at[1], other_sem.at[n]))
        leaving[n].start()
    for n in range(SIDE):
        arriving[n].wait()
        leaving.append(pltpu.make_async_copy(held.at[n], outs[n].at[0], own_sem.at[n]))
        leaving[SIDE + n].start()
    for copy in leaving:
        copy.wait()


def pair_up(places, w_out, w_other):
    hbm = pl.BlockSpec(memory_space=pltpu.HBM)
    return pl.pallas_call(
        pair_kernel,
        in_specs=[pl.BlockSpec(memory_space=pltpu.SMEM), hbm, pl.BlockSpec(memory_space=pltpu.VMEM)],
        out_specs=[hbm] * SIDE,
        out_shape=[pltpu.HBM((2, *w_other.shape[1:]), jnp.bfloat16)] * SIDE,
        scratch_shapes=[
            pltpu.VMEM(w_other.shape, jnp.bfloat16),
            pltpu.SemaphoreType.DMA((SIDE,)),
            pltpu.SemaphoreType.DMA((SIDE,)),
            pltpu.SemaphoreType.DMA((SIDE,)),
        ],
        compiler_params=pltpu.CompilerParams(vmem_limit_bytes=8 * 2**20),
        name="pair_up",
    )(places, pltpu.with_memory_space_constraint(w_out, pltpu.HBM), in_vmem(w_other))


def on_device(
    latents,
    w_query,
    w_key,
    w_value,
    w_out,
    query_gain,
    key_gain,
    mod_table,
    levels,
    span_counts,
    block_mask,
    span_order,
):
    shard_width = latents.shape[1]
    y, x, z, c = (lax.axis_index(name) for name in AXES)

    mask_low = permute(block_mask, along_queries(1))
    mask_high = permute(block_mask, along_queries(-1))
    mask_far = permute(block_mask, along_queries(2))
    mask_rows = jnp.concatenate([block_mask, mask_low, mask_high, mask_far])
    own = (latents[:HALF], latents[HALF:])
    below, above = [None, None], [None, None]
    below[0] = permute(own[0], along_z(1))
    above[1] = permute(own[1], along_z(-1))
    below[1] = permute(own[1], along_z(1))
    above[0] = permute(own[0], along_z(-1))

    places = [(z + step + SIDE) % SIDE * 2 + core for step in STEPS for core in (c, 1 - c)]
    columns = jnp.stack([(z + step + SIDE) % SIDE for step in STEPS] + [c]).astype(jnp.int32)
    modulation = lax.dynamic_index_in_dim(mod_table, levels[0], 0, keepdims=False)
    gate = lax.dynamic_slice(modulation, (2, places[0] * shard_width), (1, shard_width))

    def spans(along_x):
        return jnp.stack(
            [
                jnp.where(along_x, y * SIDE + (x + s + SIDE) % SIDE, (y + s + SIDE) % SIDE * SIDE + x)
                for s in STEPS
            ]
        )

    query_spans = spans(c == 1)
    key_spans = spans(c == 0)
    ids = jnp.arange(SIDE * SIDE, dtype=jnp.int32)
    pick_query = query_spans[:, None] == ids[None, :]
    pick_key = key_spans[:, None] == ids[None, :]
    query_rank = jnp.sum(jnp.where(pick_query, span_order[None, :], 0), axis=1)
    key_rank = jnp.sum(jnp.where(pick_key, span_order[None, :], 0), axis=1)
    counts = jnp.sum(jnp.where(pick_key, span_counts[None, :], 0), axis=1)
    w_places = jnp.stack(places).astype(jnp.int32)
    w_other = permute(take_other(w_places, w_out, shard_width), other_core)
    w_pairs = pair_up(w_places, w_out, w_other)

    far_low = permute(below[0], along_z(1))
    far_high = permute(above[1], along_z(-1))
    far_low, far_high, columns, modulation, w_pairs, mask_rows = lax.optimization_barrier(
        (far_low, far_high, columns, modulation, w_pairs, mask_rows)
    )
    far = (far_low, far_high)
    linked = jnp.sum(jnp.where(pick_key[None, :, :], mask_rows[:, None, :], 0), axis=2) == 1
    same = query_spans[:, None] == key_spans[None, :]
    allowed = ((key_rank[None, :] <= query_rank[:, None]) & (linked | same)).astype(jnp.int32).reshape(-1)
    pieces = []
    for half in range(2):
        for value in (own[half], below[half], above[half], far[half]):
            pieces += [value, permute(value, other_core)]
    w_below = permute(w_pairs[2], along_z(1))
    w_above = permute(w_pairs[1], along_z(-1))
    w_far = permute(w_pairs[3], along_z(2))
    query_own, key_own, value_own = project(
        pieces, columns, modulation, (query_gain, key_gain), (w_query, w_key, w_value)
    )

    key_low = permute(key_own, along_keys(1))
    key_high = permute(key_own, along_keys(-1))
    value_low, value_high = permute(value_own, along_keys(1)), permute(value_own, along_keys(-1))
    query_low, query_high = permute(query_own, along_queries(1)), permute(query_own, along_queries(-1))
    w_blocks = (w_pairs[0], w_below, w_above, w_far)
    key_far = permute(key_low, along_keys(1))
    value_far = permute(value_high, along_keys(-1))
    query_far = permute(query_own, along_queries(2))

    near_queries = (query_own, query_low, query_high)
    near_keys = (key_own, key_low, key_high)
    near_values = (value_own, value_low, value_high)
    state = attend_near(allowed, counts, near_queries, near_keys, near_values)
    partial = attend_far(
        allowed,
        counts,
        (*near_queries, query_far),
        (*near_keys, key_far),
        (*near_values, value_far),
        state,
    )
    sent_far = permute(partial[3], along_queries(2))
    sent_low = permute(partial[1], along_queries(-1))
    sent_high = permute(partial[2], along_queries(1))
    attended = combine((partial[0], sent_low, sent_high, sent_far))

    shared_low = permute(attended, along_z(1))
    shared_high = permute(attended, along_z(-1))
    shared_far = permute(attended, along_z(2))
    own_other = permute(attended, other_core)
    low_other = permute(shared_low, other_core)
    high_other = permute(shared_high, other_core)
    acc = output_own((attended, own_other), w_blocks[0])
    rest = (shared_low, low_other, shared_high, high_other, shared_far, permute(shared_far, other_core))
    return output_rest(acc, rest, w_blocks[1:], latents, gate)


def solution(mesh):
    fine = Mesh(mesh.devices.reshape(SIDE, SIDE, SIDE, 2), AXES)
    frame, tensor = ("y", "x"), ("z", "core")

    return jax.shard_map(
        on_device,
        mesh=fine,
        in_specs=(
            P(frame, tensor),
            P(None, tensor),
            P(None, tensor),
            P(None, tensor),
            P(tensor, None),
            P(tensor, None),
            P(tensor, None),
            P(),
            P(frame),
            P(),
            P(frame, None),
            P(),
        ),
        out_specs=P(frame, tensor),
        check_vma=False,
    )
```
